32 devices in a mesh: vol: 2 (over core), wide: 8 (over z, x), narrow: 2 (over y).
Axes of the slice: x: 2, y: 2, z: 4, core: 2. Of those that a mesh axis runs over, the one named last changes fastest.
Arguments:
- forcing: float32 [2, 4, 384, 1024], P(None, 'vol', 'narrow', 'wide'), may hold values from -180 to 180
- material_ids: int32 [4, 384, 1024], P('vol', 'narrow', 'wide'), may hold values from 0 to 7
- materials: float32 [8], replicated, may hold values from 0.5 to 2
- boundary_operator: bfloat16 [1024, 32768], P('wide', 'narrow'), may hold values from -0.03125 to 0.03125
Outputs:
- pressure: float32 [2, 4, 384, 1024], P(None, 'vol', 'narrow', 'wide')
- traction: float32 [1024, 2], P(('wide', 'narrow'), 'vol')
The draws below stay inside these ranges and needn't reach their ends.
All inputs are finite; a program needn't handle non-finite values.
Results may differ from the reference program's by a relative error of at most 0.0031.
Values may be sent and summed in bfloat16 or wider, within the bound.
No kernel may reach another device: no remote copies, remote signals or barrier semaphores. Data moves between devices by JAX's collectives and lax.ppermute only.
A program may use at most 128 MiB of HBM per device.

```python
import math
import jax
import jax.numpy as jnp
from jax import lax

K = 2
CY = 192
CX = 128
BY = 16
RY = 1
RX = 64
MAT = 8
ITERS = 2
SWEEPS = 2
NZ = 4
NY = 384
NX = 1024
NB = 32768
ROWS = 1024
N_WIDE = 8
N_NARROW = 2


def plant(result, rng, least, largest):
    extent = result.shape
    spot = [jax.random.randint(jax.random.fold_in(rng, axis), (), 0, extent[axis]) for axis in range(len(extent))]
    result = result.at[tuple(spot)].set(least)
    longest = extent.index(max(extent))
    spot[longest] = (spot[longest] + 1) % extent[longest]
    return result.at[tuple(spot)].set(largest)


def levels(key, shape, shards, smallest, largest):
    factor_of = 1.0
    for dim, shards_of in shards:
        draws = jax.random.uniform(jax.random.fold_in(jax.random.fold_in(key, 6), dim), (shards_of,), jnp.float32, smallest / len(shards), largest / len(shards))
        factor_of = factor_of * jnp.repeat(jnp.exp(draws), shape[dim] // shards_of).reshape((-1,) + (1,) * (len(shape) - 1 - dim))
    return factor_of


def bell_draw(stream_key, shape, scale, most, split=(), dtype=jnp.bfloat16):
    result = scale * jax.random.normal(stream_key, shape, jnp.float32)
    if split:
        result = result * levels(stream_key, shape, split, -0.22, 0.18)
    return jnp.clip(result, -most, most).astype(dtype)


def setup_inputs(seed: int = 0) -> dict:
    keys = jax.random.split(jax.random.key(seed), 5)
    return {
        "forcing": bell_draw(keys[0], (K, NZ, NY, NX), 30.0, 180.0, ((1, 2), (2, 2), (3, 8)), jnp.float32),
        "material_ids": plant(jax.random.randint(keys[1], (NZ, NY, NX), 0, MAT), jax.random.fold_in(keys[1], 1), 0, MAT - 1).astype(jnp.int32),
        "materials": jnp.clip(jnp.exp(jax.random.uniform(keys[2], (MAT,), jnp.float32, math.log(0.5), math.log(2.0))), 0.5, 2.0),
        "boundary_operator": bell_draw(keys[3], (ROWS, NB), NB ** -0.5, 0.03125, ((0, 8), (1, 2))),
    }


lower_edge = 0.25
upper_edge = 1.75
mass_ratio = 26.0
couple_gain = 40.0


def sweep_weights(count):
    middle = (upper_edge + lower_edge) / 2.0
    spread = (upper_edge - lower_edge) / 2.0
    center_ratio = middle / spread
    ratio_last = 1.0 / center_ratio
    weights = [(0.0, 1.0 / middle)]
    for number in range(1, count):
        ratio_next = 1.0 / (2.0 * center_ratio - ratio_last)
        weights.append((ratio_next * ratio_last, 2.0 * ratio_next / spread))
        ratio_last = ratio_next
    return weights


def box_sum(padded):
    along = padded[..., :-2] + padded[..., 1:-1] + padded[..., 2:]
    along = along[..., :-2, :] + along[..., 1:-1, :] + along[..., 2:, :]
    return along[..., :-2, :, :] + along[..., 1:-1, :, :] + along[..., 2:, :, :]


def apply_operator(padded, center, cond_pad, conductance, diagonal):
    neighbours = box_sum(padded) - center
    weighted = box_sum(padded * cond_pad) - conductance * center
    return diagonal * center - 0.5 * (conductance * neighbours + weighted)


def reference(forcing, material_ids, materials, boundary_operator):
    conductance = materials[material_ids]
    cond_pad = jnp.pad(conductance, 1)
    diagonal = 0.5 * (26.0 * conductance + (box_sum(cond_pad) - conductance)) + mass_ratio * conductance

    def relax_one(pair):
        vol_field, source = pair
        moved = jnp.zeros_like(vol_field)
        for keep_weight, gain_weight in sweep_weights(SWEEPS):
            padded = jnp.pad(vol_field, 1)
            scaled = (source - apply_operator(padded, vol_field, cond_pad, conductance, diagonal)) / diagonal
            moved = keep_weight * moved + gain_weight * scaled
            vol_field = vol_field + moved
        return vol_field

    stride = CY // BY
    pressure = jnp.zeros(forcing.shape, jnp.float32)
    source = forcing
    traction = jnp.zeros((ROWS, K), jnp.float32)
    for outer in range(ITERS):
        pressure = lax.map(relax_one, (pressure, source))
        outer_layer = pressure[:, NZ - 1].reshape(K, N_NARROW, CY, NX)[:, :, ::stride]
        trace = outer_layer.reshape(K, NB).astype(jnp.bfloat16)
        traction = jnp.dot(boundary_operator, jnp.transpose(trace), preferred_element_type=jnp.float32)
        if outer + 1 < ITERS:
            placed = traction.reshape(N_WIDE, N_NARROW, RY, RX, K).transpose(4, 1, 2, 0, 3)
            placed = jnp.pad(placed, ((0, 0), (0, 0), (0, CY - RY), (0, 0), (0, CX - RX))).reshape(K, NY, NX)
            source = forcing.at[:, NZ - 1].add(couple_gain * placed)
    return pressure, traction
```

```python
import jax
import jax.numpy as jnp
from jax import lax
from jax.experimental import pallas as pl
from jax.experimental.pallas import tpu as pltpu
from jax.sharding import PartitionSpec as P

BY = 16
HALO = 4
TILE = 8
LANES = 128

lower_edge = 0.25
upper_edge = 1.75
mass_ratio = 26.0
couple_gain = 40.0


def sweep_weights():
    middle = (upper_edge + lower_edge) / 2.0
    spread = (upper_edge - lower_edge) / 2.0
    center_ratio = middle / spread
    ratio_last = 1.0 / center_ratio
    ratio_next = 1.0 / (2.0 * center_ratio - ratio_last)
    return 1.0 / middle, ratio_next * ratio_last, 2.0 * ratio_next / spread


GAIN0, KEEP1, GAIN1 = sweep_weights()


def lookup(ids, table):
    found = jnp.zeros(ids.shape, jnp.float32)
    for number in range(table.shape[0]):
        found = jnp.where(ids == number, table[number], found)
    return found


def layer(own, other, m, v):
    return (own if m < 2 else other), (v if m % 2 == 0 else 1 - v)


def nt(a, b):
    return lax.dot_general(a, b, (((1,), (1,)), ((), ())), preferred_element_type=jnp.float32)


def rows_kernel(table, f_own, f_oth, id_own, id_oth, out):
    v, n = lax.axis_index("vol"), lax.axis_index("narrow")
    excite, _, cells_y, _ = f_own.shape
    for m in range(4):
        for e in range(excite):
            ref, li = layer(f_own, f_oth, m, v)
            out[e * 4 + m] = jnp.where(
                n == 0, ref[e, li, cells_y - HALO : cells_y, :], ref[e, li, 0:HALO, :]
            )
        ref, li = layer(id_own, id_oth, m, v)
        picked = jnp.where(n == 0, ref[li, cells_y - HALO : cells_y, :], ref[li, 0:HALO, :])
        out[excite * 4 + m] = lookup(picked, table)


def turn_kernel(table, f_own, f_oth, id_own, id_oth, got, turned, even, odd, pad):
    v, w, n = lax.axis_index("vol"), lax.axis_index("wide"), lax.axis_index("narrow")
    excite, _, cells_y, cells_x = f_own.shape
    width = pad.shape[1]
    for slab in range(excite * 4 + 4):
        m = slab % 4
        if slab < excite * 4:
            ref, li = layer(f_own, f_oth, m, v)
            block = ref[slab // 4, li]
        else:
            ref, li = layer(id_own, id_oth, m, v)
            block = lookup(ref[li], table)
        pad[slab, 0:cells_y] = block
        pad[slab, cells_y:width] = jnp.zeros((width - cells_y, cells_x), jnp.float32)
        rows = got[slab]
        pad[slab, cells_y : cells_y + HALO] = jnp.where(n == 0, rows, 0.0)
        pad[slab, width - HALO : width] = jnp.where(n == 0, 0.0, rows)
        flat = pad[slab].T
        turned[slab] = flat
        first, last = flat[0:HALO], flat[cells_x - HALO : cells_x]
        left = lax.rem(w, 2) == 0
        even[slab] = jnp.where(left, last, first)
        odd[slab] = jnp.where(left, first, last)


def sweep_kernel(turned, even, odd, pressure, trace, aux, near, ext, hh, qq, uu, cu, mv):
    v, w = lax.axis_index("vol"), lax.axis_index("wide")
    excite = pressure.shape[0]
    cells_y, cells_x = pressure.shape[2], pressure.shape[3]
    rows, width = ext.shape[1], ext.shape[2]
    right = TILE + cells_x
    left = lax.rem(w, 2) == 0
    for slab in range(ext.shape[0]):
        ext[slab, 0:TILE] = jnp.zeros((TILE, width), jnp.float32)
        ext[slab, right : right + TILE] = jnp.zeros((TILE, width), jnp.float32)
        ext[slab, TILE:right] = turned[slab]
        ext[slab, TILE - HALO : TILE] = jnp.where(left, odd[slab], even[slab])
        ext[slab, right : right + HALO] = jnp.where(left, even[slab], odd[slab])

    def box(ref, first, m):
        total = ref[first + m]
        for z in (m - 1, m + 1):
            if 0 <= z < 4:
                total = total + ref[first + z]
        total = total + pltpu.roll(total, 1, 0) + pltpu.roll(total, rows - 1, 0)
        return total + pltpu.roll(total, 1, 1) + pltpu.roll(total, width - 1, 1)

    base = excite * 4
    for m in range(4):
        c = ext[base + m]
        diagonal = 0.5 * (26.0 * c + (box(ext, base, m) - c)) + mass_ratio * c
        inverse = jnp.where(c > 0.0, 1.0 / diagonal, 0.0)
        hh[m] = 0.5 * inverse
        for e in range(excite):
            q = ext[e * 4 + m] * inverse
            qq[e * 4 + m] = q
            uu[0, e * 4 + m] = GAIN0 * q
            cu[0, e * 4 + m] = (GAIN0 * q) * c

    def residual(slot, e, m):
        u, c = uu[slot, e * 4 + m], ext[base + m]
        near_sum = box(uu.at[slot], e * 4, m) - u
        weighted = box(cu.at[slot], e * 4, m) - cu[slot, e * 4 + m]
        return (qq[e * 4 + m] - u) + hh[m] * (c * near_sum + weighted)

    for e in range(excite):
        for m in range(4):
            p = (1.0 + KEEP1) * uu[0, e * 4 + m] + GAIN1 * residual(0, e, m)
            uu[1, e * 4 + m] = p
            cu[1, e * 4 + m] = p * ext[base + m]
        for m in range(3):
            step = GAIN0 * residual(1, e, m)
            p = uu[1, e * 4 + m] + step
            mv[e * 4 + m] = step
            uu[2, e * 4 + m] = p
            cu[2, e * 4 + m] = p * ext[base + m]
        for m in range(2):
            uu[3, e * 4 + m] = (
                uu[2, e * 4 + m] + KEEP1 * mv[e * 4 + m] + GAIN1 * residual(2, e, m)
            )

    columns = 2 * excite
    r = lax.broadcasted_iota(jnp.int32, trace.shape[:1] + (width,), 0)
    lane = lax.broadcasted_iota(jnp.int32, trace.shape[:1] + (width,), 1)
    s = lax.div(r, columns)
    hit = lane == s * (cells_y // BY)
    picked = jnp.zeros(trace.shape, jnp.float32)
    for col in range(columns):
        e, late = col % excite, col >= excite
        match = hit & (lax.rem(r, columns) == col)
        if late:
            match = match & (s > 0)
        values = uu[3 if late else 1, e * 4, TILE:right].astype(jnp.bfloat16)
        picked = picked + nt(jnp.where(match, 1.0, 0.0).astype(jnp.bfloat16), values)
    trace[...] = picked.astype(jnp.bfloat16)

    aux[...] = jnp.zeros(aux.shape, jnp.float32)
    near[...] = jnp.zeros(near.shape, jnp.float32)
    for m in range(2):
        li = v if m == 0 else 1 - v
        for e in range(excite):
            back = uu[3, e * 4 + m, TILE:right].T
            pressure[e, li] = back[0:cells_y]
            if m == 0:
                aux[e : e + 1] = back[0:1]
        for k, source in enumerate((ext[base + m, TILE:right], hh[m, TILE:right])):
            back = source.T
            for i, y in enumerate((0, 1, cells_y - 1)):
                row = 6 * k + 3 * m + i
                near[row : row + 1] = back[y : y + 1]
            if m == 0:
                aux[excite + k : excite + k + 1] = back[0:1]


def product_kernel(blocks, operator, aux, out):
    w = lax.axis_index("wide")
    count = blocks.shape[0]
    tile_rows = operator.shape[0]
    odd = lax.rem(w, 2)

    def pair(p, sums):
        base = lax.div(w ^ (2 * p), 2) * 2
        low, high = blocks[2 * p + odd], blocks[2 * p + 1 - odd]
        both = jnp.concatenate([low, high], axis=1)
        sums = list(sums)
        for s in range(BY):
            start = pl.multiple_of(s * count * LANES + base * LANES, LANES)
            group = s // 4 * 16
            sums[s % 4] = sums[s % 4] + nt(both[group : group + 16], operator[:, pl.ds(start, 2 * LANES)])
        return tuple(sums)

    zero = jnp.zeros((16, tile_rows), jnp.float32)
    sums = lax.fori_loop(0, count // 2, pair, (zero,) * 4)
    r = lax.broadcasted_iota(jnp.int32, zero.shape, 0)
    total = zero
    for q in range(4):
        total = total + jnp.where((r >= 4 * q) & (r < 4 * q + 4), sums[q], 0.0)
    total = total[0:8] + total[8:16]
    total = total + pltpu.roll(total, 4, 0)
    r = lax.broadcasted_iota(jnp.int32, total.shape, 0)
    out[...] = jnp.where(r < 4, total, pltpu.roll(aux[...], 4, 0))


def couple_kernel(blocks, mine, theirs, traction, fix, flat, save):
    v, w, n = lax.axis_index("vol"), lax.axis_index("wide"), lax.axis_index("narrow")
    count = blocks.shape[0]
    excite = 2
    targets = mine.shape[0]
    for j in range(count):
        flat[pl.ds(j * 16, 8), :] = blocks[w ^ j, 0]
        flat[pl.ds(j * 16 + 8, 8), :] = blocks[w ^ j, 1]

    def field(k, r):
        return flat[pl.ds(k * 8 + r, count, stride=16), :]

    lane = lax.broadcasted_iota(jnp.int32, (count, LANES), 1)
    sub = lax.broadcasted_iota(jnp.int32, (count, LANES), 0)

    def before(a):
        return pltpu.roll(a, 1, 1)

    def after(a):
        moved = pltpu.roll(a, LANES - 1, 1)
        following = jnp.where(sub == count - 1, 0.0, pltpu.roll(moved, count - 1, 0))
        return jnp.where(lane == LANES - 1, following, moved)

    own = (1.0 + KEEP1) * GAIN0 + GAIN1 - GAIN1 * GAIN0
    sides = []
    for k in range(2):
        c, h = field(k, 4 + excite), field(k, 5 + excite)
        rows = []
        for e in range(excite):
            t = field(0, e) + field(1, e)
            if k:
                t = pltpu.roll(t, LANES - targets, 1)
            t = jnp.where(lane < targets, t, 0.0)
            u = (2.0 * couple_gain) * h * t
            cu = c * u
            around, c_around = before(u) + after(u), before(cu) + after(cu)
            change = own * u + (GAIN0 * GAIN1) * h * (c * around + c_around)
            save[k, 0, e] = change
            save[k, 1, e] = around + u
            save[k, 2, e] = c_around + cu
            rows.append(field(k, 4 + e) + change)
        sides.append(rows)

    groups = count // 8
    total = jnp.zeros((16, targets), jnp.float32)
    r = lax.broadcasted_iota(jnp.int32, total.shape, 0)
    for g in range(groups):
        both = [
            jnp.concatenate([sides[k][e][8 * g : 8 * g + 8] for e in range(excite)], axis=0)
            for k in range(2)
        ]
        for ref, left in (
            (mine, jnp.where(n == 0, both[0], both[1])),
            (theirs, jnp.where(n == 0, both[1], both[0])),
        ):
            left = left.astype(jnp.bfloat16)
            for j in range(8):
                part = nt(left, ref[:, (8 * g + j) * LANES : (8 * g + j + 1) * LANES])
                total = total + jnp.where((r & 7) == j, part, 0.0)
    first = blocks[0, 0] + blocks[0, 1]
    first = jnp.where(n == 0, first, pltpu.roll(first, LANES - targets, 1))
    traction[...] = jnp.zeros(traction.shape, jnp.float32)
    for e in range(excite):
        traction[e : e + 1, 0:targets] = (
            jnp.sum(total[8 * e : 8 * e + 8], axis=0, keepdims=True)
            + first[2 + e : 3 + e, 0:targets]
        )

    top = v == lax.axis_size("vol") - 1
    fix[...] = jnp.zeros(fix.shape, jnp.float32)
    for e in range(excite):
        for i in range(3):
            row = 2 * i + e
            fix[row : row + 1] = jnp.where(top, save[n, i, e, pl.ds(w, 1), :], 0.0)
        for i in range(1, 3):
            row = 4 + 2 * i + e
            fix[row : row + 1] = jnp.where(
                top & (n == 0), save[1, i, e, pl.ds(w, 1), :], 0.0
            )


def mend_kernel(pressure, near, fix, out):
    v = lax.axis_index("vol")
    excite, _, cells_y, cells_x = pressure.shape
    r = lax.broadcasted_iota(jnp.int32, (8, cells_x), 0)
    out[...] = pressure[...]
    for e in range(excite):
        for m in range(2):
            li = v if m == 0 else 1 - v

            def change(i, a, b):
                c, h = near[3 * m + i : 3 * m + i + 1], near[6 + 3 * m + i : 7 + 3 * m + i]
                return (GAIN0 * GAIN1) * h * (c * fix[a + e : a + e + 1] + fix[b + e : b + e + 1])

            row0 = fix[e : e + 1] if m == 0 else change(0, 2, 4)
            delta = jnp.where(r == 0, row0, jnp.where(r == 1, change(1, 2, 4), 0.0))
            out[e, li, 0:8] = pressure[e, li, 0:8] + delta
            delta = jnp.where(r == 7, change(2, 6, 8), 0.0)
            out[e, li, cells_y - 8 : cells_y] = pressure[e, li, cells_y - 8 : cells_y] + delta


def local(forcing, material_ids, materials, boundary_operator):
    vols, wides, narrows = (lax.axis_size(a) for a in ("vol", "wide", "narrow"))
    v, w, n = lax.axis_index("vol"), lax.axis_index("wide"), lax.axis_index("narrow")
    excite, layers, cells_y, cells_x = forcing.shape
    assert (vols, narrows, excite, layers, cells_x) == (2, 2, 2, 2, LANES)
    assert wides % 8 == 0 and wides & (wides - 1) == 0
    tile_rows = boundary_operator.shape[0]
    targets = tile_rows // narrows
    assert tile_rows == LANES and BY * 2 * excite == 64
    width = -(-(cells_y + 2 * HALO) // LANES) * LANES
    slabs = 4 * excite + 4
    f32, bf16 = jnp.float32, jnp.bfloat16
    everyone = ("vol", "wide", "narrow")
    vmem, smem = pl.BlockSpec(memory_space=pltpu.VMEM), pl.BlockSpec(memory_space=pltpu.SMEM)

    def call(kernel, shapes, specs, scratch=()):
        return pl.pallas_call(
            kernel,
            out_shape=[jax.ShapeDtypeStruct(*s) for s in shapes],
            in_specs=specs,
            out_specs=[vmem] * len(shapes),
            scratch_shapes=list(scratch),
        )

    def swap(x, axis):
        return lax.ppermute(x, axis, [(0, 1), (1, 0)])

    def number(a, b, c):
        return (a * wides + b) * narrows + c

    def top_permute(x, partner):
        return lax.ppermute(
            x,
            everyone,
            [
                (number(vols - 1, b, c), number(vols - 1, *partner(b, c)))
                for b in range(wides)
                for c in range(narrows)
            ],
        )

    f_other, id_other = swap(forcing, "vol"), swap(material_ids, "vol")
    cells = (forcing, f_other, material_ids, id_other)
    (edge,) = call(rows_kernel, [((slabs, HALO, cells_x), f32)], [smem] + [vmem] * 4)(
        materials, *cells
    )
    edge = swap(edge, "narrow")
    head = boundary_operator[:, : wides * LANES]
    mine = lax.dynamic_slice_in_dim(head, n * targets, targets, 0)
    theirs = swap(lax.dynamic_slice_in_dim(head, (1 - n) * targets, targets, 0), "narrow")
    turned, even, odd = call(
        turn_kernel,
        [((slabs, cells_x, width), f32)] + [((slabs, HALO, width), f32)] * 2,
        [smem] + [vmem] * 5,
        [pltpu.VMEM((slabs, width, cells_x), f32)],
    )(materials, *cells, edge)
    even_pairs = [(i, i ^ 1) for i in range(wides)]
    odd_pairs = [(i, i + 1 if i % 2 else i - 1) for i in range(1, wides - 1)]
    even, odd = lax.ppermute(even, "wide", even_pairs), lax.ppermute(odd, "wide", odd_pairs)
    rows = cells_x + 2 * TILE
    full = (rows, width)
    pressure, trace, aux, near = call(
        sweep_kernel,
        [
            (forcing.shape, f32),
            ((BY * 2 * excite, cells_x), bf16),
            ((8, cells_x), f32),
            ((16, cells_x), f32),
        ],
        [vmem] * 3,
        [
            pltpu.VMEM((slabs,) + full, f32),
            pltpu.VMEM((4,) + full, f32),
            pltpu.VMEM((4 * excite,) + full, f32),
            pltpu.VMEM((4, 4 * excite) + full, f32),
            pltpu.VMEM((3, 4 * excite) + full, f32),
            pltpu.VMEM((4 * excite,) + full, f32),
        ],
    )(turned, even, odd)

    def gather(block):
        step = 1
        while step < wides:
            other = top_permute(block, lambda b, c: (b ^ step, c))
            block = jnp.concatenate([block, other], axis=0)
            step *= 2
        return block

    blocks = gather(trace[None])
    (sums,) = call(product_kernel, [((8, tile_rows), f32)], [vmem] * 3)(
        blocks, boundary_operator, aux
    )
    other = top_permute(sums, lambda b, c: (b, 1 - c))
    pair = jnp.stack([jnp.where(n == 0, sums, other), jnp.where(n == 0, other, sums)])
    blocks = gather(pair[None])
    traction, fix = call(
        couple_kernel,
        [((8, LANES), f32), ((16, cells_x), f32)],
        [vmem] * 3,
        [pltpu.VMEM((wides * 16, LANES), f32), pltpu.VMEM((2, 3, excite, wides, LANES), f32)],
    )(blocks, mine, theirs)
    (pressure,) = call(mend_kernel, [(forcing.shape, f32)], [vmem] * 3)(pressure, near, fix)
    lower = lax.ppermute(traction[0:1, :targets], "vol", [(1, 0)])
    column = jnp.where(v == vols - 1, traction[1:2, :targets], lower)
    return pressure, column.reshape(targets, 1)


def solution(mesh):
    placed = (
        P(None, "vol", "narrow", "wide"),
        P("vol", "narrow", "wide"),
        P(),
        P("wide", "narrow"),
    )
    return jax.shard_map(
        local,
        mesh=mesh,
        in_specs=placed,
        out_specs=(P(None, "vol", "narrow", "wide"), P(("wide", "narrow"), "vol")),
        check_vma=False,
    )
```

```python
import jax
import jax.numpy as jnp
from jax import lax
from jax.experimental import pallas as pl
from jax.experimental.pallas import tpu as pltpu
from jax.sharding import PartitionSpec as P

BY = 16
HALO = 4
TILE = 8
LANES = 128

lower_edge = 0.25
upper_edge = 1.75
mass_ratio = 26.0
couple_gain = 40.0


def sweep_weights():
    middle = (upper_edge + lower_edge) / 2.0
    spread = (upper_edge - lower_edge) / 2.0
    center_ratio = middle / spread
    ratio_last = 1.0 / center_ratio
    ratio_next = 1.0 / (2.0 * center_ratio - ratio_last)
    return 1.0 / middle, ratio_next * ratio_last, 2.0 * ratio_next / spread


GAIN0, KEEP1, GAIN1 = sweep_weights()


def lookup(ids, table):
    found = jnp.zeros(ids.shape, jnp.float32)
    for number in range(table.shape[0]):
        found = jnp.where(ids == number, table[number], found)
    return found


def layer(own, other, m, v):
    return (own if m < 2 else other), (v if m % 2 == 0 else 1 - v)


def nt(a, b):
    return lax.dot_general(a, b, (((1,), (1,)), ((), ())), preferred_element_type=jnp.float32)


def rows_kernel(table, f_own, f_oth, id_own, id_oth, out):
    v, n = lax.axis_index("vol"), lax.axis_index("narrow")
    excite, _, cells_y, _ = f_own.shape
    for m in range(4):
        for e in range(excite):
            ref, li = layer(f_own, f_oth, m, v)
            out[e * 4 + m] = jnp.where(
                n == 0, ref[e, li, cells_y - HALO : cells_y, :], ref[e, li, 0:HALO, :]
            )
        ref, li = layer(id_own, id_oth, m, v)
        picked = jnp.where(n == 0, ref[li, cells_y - HALO : cells_y, :], ref[li, 0:HALO, :])
        out[excite * 4 + m] = lookup(picked, table)


def turn_kernel(table, f_own, f_oth, id_own, id_oth, got, turned, even, odd, pad):
    v, w, n = lax.axis_index("vol"), lax.axis_index("wide"), lax.axis_index("narrow")
    excite, _, cells_y, cells_x = f_own.shape
    width = pad.shape[1]
    for slab in range(excite * 4 + 4):
        m = slab % 4
        if slab < excite * 4:
            ref, li = layer(f_own, f_oth, m, v)
            block = ref[slab // 4, li]
        else:
            ref, li = layer(id_own, id_oth, m, v)
            block = lookup(ref[li], table)
        pad[slab, 0:cells_y] = block
        pad[slab, cells_y:width] = jnp.zeros((width - cells_y, cells_x), jnp.float32)
        rows = got[slab]
        pad[slab, cells_y : cells_y + HALO] = jnp.where(n == 0, rows, 0.0)
        pad[slab, width - HALO : width] = jnp.where(n == 0, 0.0, rows)
        flat = pad[slab].T
        turned[slab] = flat
        first, last = flat[0:HALO], flat[cells_x - HALO : cells_x]
        left = lax.rem(w, 2) == 0
        even[slab] = jnp.where(left, last, first)
        odd[slab] = jnp.where(left, first, last)


def sweep_kernel(turned, even, odd, pressure, trace, aux, near, ext, hh, qq, uu, cu, mv):
    v, w = lax.axis_index("vol"), lax.axis_index("wide")
    inner = (w > 0) & (w < lax.axis_size("wide") - 1)
    excite = pressure.shape[0]
    cells_y, cells_x = pressure.shape[2], pressure.shape[3]
    rows, width = ext.shape[1], ext.shape[2]
    right = TILE + cells_x
    left = lax.rem(w, 2) == 0
    for slab in range(ext.shape[0]):
        ext[slab, 0:TILE] = jnp.zeros((TILE, width), jnp.float32)
        ext[slab, right : right + TILE] = jnp.zeros((TILE, width), jnp.float32)
        ext[slab, TILE:right] = turned[slab]
        outer = jnp.where(inner, odd[slab], 0.0)
        ext[slab, TILE - HALO : TILE] = jnp.where(left, outer, even[slab])
        ext[slab, right : right + HALO] = jnp.where(left, even[slab], outer)

    def box(ref, first, m):
        total = ref[first + m]
        for z in (m - 1, m + 1):
            if 0 <= z < 4:
                total = total + ref[first + z]
        total = total + pltpu.roll(total, 1, 0) + pltpu.roll(total, rows - 1, 0)
        return total + pltpu.roll(total, 1, 1) + pltpu.roll(total, width - 1, 1)

    base = excite * 4
    for m in range(4):
        c = ext[base + m]
        diagonal = 0.5 * (26.0 * c + (box(ext, base, m) - c)) + mass_ratio * c
        inverse = jnp.where(c > 0.0, 1.0 / diagonal, 0.0)
        hh[m] = 0.5 * inverse
        for e in range(excite):
            q = ext[e * 4 + m] * inverse
            qq[e * 4 + m] = q
            uu[0, e * 4 + m] = GAIN0 * q
            cu[0, e * 4 + m] = (GAIN0 * q) * c

    def residual(slot, e, m):
        u, c = uu[slot, e * 4 + m], ext[base + m]
        near_sum = box(uu.at[slot], e * 4, m) - u
        weighted = box(cu.at[slot], e * 4, m) - cu[slot, e * 4 + m]
        return (qq[e * 4 + m] - u) + hh[m] * (c * near_sum + weighted)

    for e in range(excite):
        for m in range(4):
            p = (1.0 + KEEP1) * uu[0, e * 4 + m] + GAIN1 * residual(0, e, m)
            uu[1, e * 4 + m] = p
            cu[1, e * 4 + m] = p * ext[base + m]
        for m in range(3):
            step = GAIN0 * residual(1, e, m)
            p = uu[1, e * 4 + m] + step
            mv[e * 4 + m] = step
            uu[2, e * 4 + m] = p
            cu[2, e * 4 + m] = p * ext[base + m]
        for m in range(2):
            uu[3, e * 4 + m] = (
                uu[2, e * 4 + m] + KEEP1 * mv[e * 4 + m] + GAIN1 * residual(2, e, m)
            )

    columns = 2 * excite
    r = lax.broadcasted_iota(jnp.int32, (trace.shape[1], width), 0)
    lane = lax.broadcasted_iota(jnp.int32, (trace.shape[1], width), 1)
    s = lax.div(r, columns)
    hit = lane == s * (cells_y // BY)
    picked = jnp.zeros(trace.shape[1:], jnp.float32)
    for col in range(columns):
        e, late = col % excite, col >= excite
        match = hit & (lax.rem(r, columns) == col)
        if late:
            match = match & (s > 0)
        values = uu[3 if late else 1, e * 4, TILE:right].astype(jnp.bfloat16)
        picked = picked + nt(jnp.where(match, 1.0, 0.0).astype(jnp.bfloat16), values)
    for j in range(trace.shape[0]):
        trace[j] = picked.astype(jnp.bfloat16)

    aux[...] = jnp.zeros(aux.shape, jnp.float32)
    near[...] = jnp.zeros(near.shape, jnp.float32)
    for m in range(2):
        li = v if m == 0 else 1 - v
        for e in range(excite):
            back = uu[3, e * 4 + m, TILE:right].T
            pressure[e, li] = back[0:cells_y]
            if m == 0:
                aux[e : e + 1] = back[0:1]
        for k, source in enumerate((ext[base + m, TILE:right], hh[m, TILE:right])):
            back = source.T
            for i, y in enumerate((0, 1, cells_y - 1)):
                row = 6 * k + 3 * m + i
                near[row : row + 1] = back[y : y + 1]
            if m == 0:
                aux[excite + k : excite + k + 1] = back[0:1]


def product_kernel(blocks, operator, aux, out):
    count = blocks.shape[0]
    tile_rows = operator.shape[0]

    def pair(p, sums):
        both = jnp.concatenate([blocks[2 * p], blocks[2 * p + 1]], axis=1)
        sums = list(sums)
        for s in range(BY):
            start = pl.multiple_of(s * count * LANES + p * (2 * LANES), 2 * LANES)
            group = s // 4 * 16
            sums[s % 4] = sums[s % 4] + nt(both[group : group + 16], operator[:, pl.ds(start, 2 * LANES)])
        return tuple(sums)

    zero = jnp.zeros((16, tile_rows), jnp.float32)
    sums = lax.fori_loop(0, count // 2, pair, (zero,) * 4)
    r = lax.broadcasted_iota(jnp.int32, zero.shape, 0)
    total = zero
    for q in range(4):
        total = total + jnp.where((r >= 4 * q) & (r < 4 * q + 4), sums[q], 0.0)
    total = total[0:8] + total[8:16]
    total = total + pltpu.roll(total, 4, 0)
    r = lax.broadcasted_iota(jnp.int32, total.shape, 0)
    total = jnp.where(r < 4, total, pltpu.roll(aux[...], 4, 0))
    for j in range(out.shape[0]):
        out[j] = total


def couple_kernel(flat, mine, theirs, traction, fix, save):
    w, n = lax.axis_index("wide"), lax.axis_index("narrow")
    count = flat.shape[0] // 16
    excite = 2
    targets = mine.shape[0]

    def field(k, r):
        return flat[pl.ds(k * 8 + r, count, stride=16), :]

    lane = lax.broadcasted_iota(jnp.int32, (count, LANES), 1)
    sub = lax.broadcasted_iota(jnp.int32, (count, LANES), 0)

    def before(a):
        return pltpu.roll(a, 1, 1)

    def after(a):
        moved = pltpu.roll(a, LANES - 1, 1)
        following = jnp.where(sub == count - 1, 0.0, pltpu.roll(moved, count - 1, 0))
        return jnp.where(lane == LANES - 1, following, moved)

    own = (1.0 + KEEP1) * GAIN0 + GAIN1 - GAIN1 * GAIN0
    sides = []
    for k in range(2):
        c, h = field(k, 4 + excite), field(k, 5 + excite)
        rows = []
        for e in range(excite):
            t = field(0, e) + field(1, e)
            if k:
                t = pltpu.roll(t, LANES - targets, 1)
            t = jnp.where(lane < targets, t, 0.0)
            u = (2.0 * couple_gain) * h * t
            cu = c * u
            around, c_around = before(u) + after(u), before(cu) + after(cu)
            change = own * u + (GAIN0 * GAIN1) * h * (c * around + c_around)
            save[k, 0, e] = change
            save[k, 1, e] = around + u
            save[k, 2, e] = c_around + cu
            rows.append(field(k, 4 + e) + change)
        sides.append(rows)

    groups = count // 8
    total = jnp.zeros((16, targets), jnp.float32)
    r = lax.broadcasted_iota(jnp.int32, total.shape, 0)
    for g in range(groups):
        both = [
            jnp.concatenate([sides[k][e][8 * g : 8 * g + 8] for e in range(excite)], axis=0)
            for k in range(2)
        ]
        for ref, left in (
            (mine, jnp.where(n == 0, both[0], both[1])),
            (theirs, jnp.where(n == 0, both[1], both[0])),
        ):
            left = left.astype(jnp.bfloat16)
            for j in range(8):
                part = nt(left, ref[:, (8 * g + j) * LANES : (8 * g + j + 1) * LANES])
                total = total + jnp.where((r & 7) == j, part, 0.0)
    first = flat[pl.ds(pl.multiple_of(w * 16, 16), 8), :] + flat[pl.ds(pl.multiple_of(w * 16 + 8, 8), 8), :]
    first = jnp.where(n == 0, first, pltpu.roll(first, LANES - targets, 1))
    traction[...] = jnp.zeros(traction.shape, jnp.float32)
    for e in range(excite):
        traction[e : e + 1, 0:targets] = (
            jnp.sum(total[8 * e : 8 * e + 8], axis=0, keepdims=True)
            + first[2 + e : 3 + e, 0:targets]
        )

    fix[...] = jnp.zeros(fix.shape, jnp.float32)
    for e in range(excite):
        for i in range(3):
            row = 2 * i + e
            fix[row : row + 1] = save[n, i, e, pl.ds(w, 1), :]
        for i in range(1, 3):
            row = 4 + 2 * i + e
            fix[row : row + 1] = jnp.where(n == 0, save[1, i, e, pl.ds(w, 1), :], 0.0)


def mend_kernel(pressure, near, fix, out):
    v = lax.axis_index("vol")
    excite, _, cells_y, cells_x = pressure.shape
    r = lax.broadcasted_iota(jnp.int32, (8, cells_x), 0)
    out[...] = pressure[...]
    for e in range(excite):
        for m in range(2):
            li = v if m == 0 else 1 - v

            def change(i, a, b):
                c, h = near[3 * m + i : 3 * m + i + 1], near[6 + 3 * m + i : 7 + 3 * m + i]
                return (GAIN0 * GAIN1) * h * (c * fix[a + e : a + e + 1] + fix[b + e : b + e + 1])

            row0 = fix[e : e + 1] if m == 0 else change(0, 2, 4)
            delta = jnp.where(r == 0, row0, jnp.where(r == 1, change(1, 2, 4), 0.0))
            out[e, li, 0:8] = pressure[e, li, 0:8] + delta
            delta = jnp.where(r == 7, change(2, 6, 8), 0.0)
            out[e, li, cells_y - 8 : cells_y] = pressure[e, li, cells_y - 8 : cells_y] + delta


def local(forcing, material_ids, materials, boundary_operator):
    vols, wides, narrows = (lax.axis_size(a) for a in ("vol", "wide", "narrow"))
    v, w, n = lax.axis_index("vol"), lax.axis_index("wide"), lax.axis_index("narrow")
    excite, layers, cells_y, cells_x = forcing.shape
    assert (vols, narrows, excite, layers, cells_x) == (2, 2, 2, 2, LANES)
    assert wides % 8 == 0 and wides & (wides - 1) == 0
    tile_rows = boundary_operator.shape[0]
    targets = tile_rows // narrows
    assert tile_rows == LANES and BY * 2 * excite == 64
    width = -(-(cells_y + 2 * HALO) // LANES) * LANES
    slabs = 4 * excite + 4
    f32, bf16 = jnp.float32, jnp.bfloat16
    everyone = ("vol", "wide", "narrow")
    vmem, smem = pl.BlockSpec(memory_space=pltpu.VMEM), pl.BlockSpec(memory_space=pltpu.SMEM)

    def call(kernel, shapes, specs, scratch=(), limit=4):
        return pl.pallas_call(
            kernel,
            out_shape=[jax.ShapeDtypeStruct(*s) for s in shapes],
            in_specs=specs,
            out_specs=[vmem] * len(shapes),
            scratch_shapes=list(scratch),
            compiler_params=pltpu.CompilerParams(vmem_limit_bytes=limit * 2**20),
        )

    def swap(x, axis):
        return lax.ppermute(x, axis, [(0, 1), (1, 0)])

    def number(a, b, c):
        return (a * wides + b) * narrows + c

    f_other, id_other = swap(forcing, "vol"), swap(material_ids, "vol")
    cells = (forcing, f_other, material_ids, id_other)
    (edge,) = call(rows_kernel, [((slabs, HALO, cells_x), f32)], [smem] + [vmem] * 4)(
        materials, *cells
    )
    edge = swap(edge, "narrow")
    head = boundary_operator[:, : wides * LANES]
    mine = lax.dynamic_slice_in_dim(head, n * targets, targets, 0)
    theirs = swap(lax.dynamic_slice_in_dim(head, (1 - n) * targets, targets, 0), "narrow")
    turned, even, odd = call(
        turn_kernel,
        [((slabs, cells_x, width), f32)] + [((slabs, HALO, width), f32)] * 2,
        [smem] + [vmem] * 5,
        [pltpu.VMEM((slabs, width, cells_x), f32)],
        8,
    )(materials, *cells, edge)
    even = lax.ppermute(even, "wide", [(i, i ^ 1) for i in range(wides)])
    odd_pairs = []
    for a in range(vols):
        for b in range(wides):
            for c in range(narrows):
                far = b + 1 if b % 2 else b - 1
                there = (far, c) if 0 <= far < wides else (b, 1 - c)
                odd_pairs.append((number(a, b, c), number(a, *there)))
    odd = lax.ppermute(odd, everyone, odd_pairs)
    rows = cells_x + 2 * TILE
    full = (rows, width)
    pressure, trace, aux, near = call(
        sweep_kernel,
        [
            (forcing.shape, f32),
            ((wides, BY * 2 * excite, cells_x), bf16),
            ((8, cells_x), f32),
            ((16, cells_x), f32),
        ],
        [vmem] * 3,
        [
            pltpu.VMEM((slabs,) + full, f32),
            pltpu.VMEM((4,) + full, f32),
            pltpu.VMEM((4 * excite,) + full, f32),
            pltpu.VMEM((4, 4 * excite) + full, f32),
            pltpu.VMEM((3, 4 * excite) + full, f32),
            pltpu.VMEM((4 * excite,) + full, f32),
        ],
        24,
    )(turned, even, odd)

    def couple(trace, aux, boundary_operator, mine, theirs):
        blocks = lax.all_to_all(trace, "wide", 0, 0)
        (sums,) = call(product_kernel, [((wides * narrows, 8, tile_rows), f32)], [vmem] * 3, (), 24)(
            blocks, boundary_operator, aux
        )
        blocks = lax.all_to_all(sums, ("wide", "narrow"), 0, 0)
        return tuple(call(
            couple_kernel,
            [((8, LANES), f32), ((16, cells_x), f32)],
            [vmem] * 3,
            [pltpu.VMEM((2, 3, excite, wides, LANES), f32)],
        )(blocks.reshape(wides * narrows * 8, LANES), mine, theirs))

    def nothing(*_):
        return jnp.zeros((8, LANES), f32), jnp.zeros((16, cells_x), f32)

    traction, fix = lax.cond(
        v == vols - 1, couple, nothing, trace, aux, boundary_operator, mine, theirs
    )
    (pressure,) = call(mend_kernel, [(forcing.shape, f32)], [vmem] * 3)(pressure, near, fix)
    column = traction[0:2, :targets]
    lower = swap(column, "vol")
    column = jnp.where(v == vols - 1, column[1:2], lower[0:1])
    return pressure, column.reshape(targets, 1)


def solution(mesh):
    placed = (
        P(None, "vol", "narrow", "wide"),
        P("vol", "narrow", "wide"),
        P(),
        P("wide", "narrow"),
    )
    return jax.shard_map(
        local,
        mesh=mesh,
        in_specs=placed,
        out_specs=(P(None, "vol", "narrow", "wide"), P(("wide", "narrow"), "vol")),
        check_vma=False,
    )
```

```python
import functools

import jax
import jax.numpy as jnp
from jax import lax
from jax.experimental import pallas as pl
from jax.experimental.pallas import tpu as pltpu
from jax.sharding import PartitionSpec as P

BY = 16
HALO = 4
TILE = 8
LANES = 128

lower_edge = 0.25
upper_edge = 1.75
mass_ratio = 26.0
couple_gain = 40.0


def sweep_weights():
    middle = (upper_edge + lower_edge) / 2.0
    spread = (upper_edge - lower_edge) / 2.0
    center_ratio = middle / spread
    ratio_last = 1.0 / center_ratio
    ratio_next = 1.0 / (2.0 * center_ratio - ratio_last)
    return 1.0 / middle, ratio_next * ratio_last, 2.0 * ratio_next / spread


GAIN0, KEEP1, GAIN1 = sweep_weights()


def lookup(ids, table):
    found = jnp.zeros(ids.shape, jnp.float32)
    for number in range(table.shape[0]):
        found = jnp.where(ids == number, table[number], found)
    return found


def nt(a, b):
    return lax.dot_general(a, b, (((1,), (1,)), ((), ())), preferred_element_type=jnp.float32)


def inner_first(k, v):
    return v if k % 2 == 0 else 1 - v


def turn(block, out, slab):
    cells_y, cells_x = block.shape
    behind = jnp.zeros((out.shape[2] - cells_y, cells_x), jnp.float32)
    out[slab] = jnp.concatenate([block, behind], axis=0).T


def edge_rows(n, ref, *at):
    cells_y = ref.shape[-2]
    return jnp.where(
        n == 0, ref[*at, cells_y - HALO : cells_y, :], ref[*at, 0:HALO, :]
    )


def own_kernel(
    table, forcing, ids, operator, turned, edge, spread, sent, kept, f_in, id_in, table_in, sems
):
    v, n = lax.axis_index("vol"), lax.axis_index("narrow")
    targets, columns = sent.shape
    copies = [
        pltpu.make_async_copy(table, table_in, sems.at[0]),
        pltpu.make_async_copy(ids, id_in, sems.at[1]),
        pltpu.make_async_copy(forcing, f_in, sems.at[2]),
    ]
    for row, out in ((1 - n, sent), (n, kept)):
        rows = pl.ds(pl.multiple_of(row * targets, targets), targets)
        source = operator.at[rows, 0:columns]
        copies.append(pltpu.make_async_copy(source, out, sems.at[len(copies)]))
    for copy in copies:
        copy.start()
    excite = forcing.shape[0]
    copies[0].wait()
    for k in range(spread.shape[0]):
        spread[k : k + 1] = jnp.full((1, spread.shape[1]), table_in[k], jnp.float32)
    copies[1].wait()
    for m in range(2):
        li = inner_first(m, v)
        edge[2 * excite + m] = lookup(edge_rows(n, id_in, li), table_in)
        turn(lookup(id_in[li], table_in), turned, 2 * excite + m)
    copies[2].wait()
    for e in range(excite):
        for m in range(2):
            li = inner_first(m, v)
            edge[2 * e + m] = edge_rows(n, f_in, e, li)
            turn(f_in[e, li], turned, 2 * e + m)
    copies[3].wait()
    copies[4].wait()


def look_rows(ids, spread):
    found = jnp.zeros(ids.shape, jnp.float32)
    for number in range(spread.shape[0]):
        found = jnp.where(ids == number, spread[number : number + 1], found)
    return found


def edge_kernel(forcing, ids, own_edge, spread, edge):
    v, n = lax.axis_index("vol"), lax.axis_index("narrow")
    excite = forcing.shape[0]
    half = own_edge.shape[0]
    edge[0:half] = own_edge[...]
    for m in range(2):
        li = inner_first(m, v)
        edge[half + 2 * excite + m] = look_rows(edge_rows(n, ids, li), spread)
        for e in range(excite):
            edge[half + 2 * e + m] = edge_rows(n, forcing, e, li)


def other_kernel(forcing, ids, spread, turned):
    v = lax.axis_index("vol")
    excite = forcing.shape[0]
    for m in range(2):
        li = inner_first(m, v)
        turn(look_rows(ids[li], spread), turned, 2 * excite + m)
        for e in range(excite):
            turn(forcing[e, li], turned, 2 * e + m)


def turned_edge(got):
    slabs, halo, cells_x = got.shape
    rows = jnp.concatenate([got[k] for k in range(slabs)], axis=0)
    behind = jnp.zeros((LANES - slabs * halo, cells_x), jnp.float32)
    return jnp.concatenate([rows, behind], axis=0).T


def with_edge(last, rows, slab, used, n):
    base = jnp.where(n == 0, used, LANES - HALO)
    lane = lax.broadcasted_iota(jnp.int32, last.shape, 1)
    moved = pltpu.roll(rows, lax.rem(base - HALO * slab + LANES, LANES), 1)
    return jnp.where((lane >= base) & (lane < base + HALO), moved, last)


def side_kernel(used, own, other, got, even, odd, turned):
    w, n = lax.axis_index("wide"), lax.axis_index("narrow")
    half = own.shape[0]
    cells_x, width = own.shape[1], own.shape[2]
    rows = turned_edge(got)
    turned[...] = rows
    left = lax.rem(w, 2) == 0
    for slab in range(2 * half):
        ref, k = (own, slab) if slab < half else (other, slab - half)
        sides = []
        for at in (0, cells_x - TILE):
            last = with_edge(ref[k, at : at + TILE, width - LANES :], rows[at : at + TILE], slab, used, n)
            sides.append(jnp.concatenate([ref[k, at : at + TILE, : width - LANES], last], axis=1))
        first, last = sides[0][0:HALO], sides[1][TILE - HALO :]
        even[slab] = jnp.where(left, last, first)
        odd[slab] = jnp.where(left, first, last)


def order(excite):
    half = 2 * excite + 2
    kinds = list(range(excite)) + [excite]
    return [(0 if m < 2 else half) + 2 * k + m % 2 for k in kinds for m in range(4)]


def extend_kernel(used, own, other, turned, even, ext):
    n = lax.axis_index("narrow")
    half = own.shape[0]
    cells_x, width = own.shape[1], own.shape[2]
    right = TILE + cells_x
    left = lax.rem(lax.axis_index("wide"), 2) == 0
    rows = turned[...]
    for place, slab in enumerate(order((half - 2) // 2)):
        ref, k = (own, slab) if slab < half else (other, slab - half)
        ext[place, 0:TILE] = jnp.zeros((TILE, width), jnp.float32)
        ext[place, right : right + TILE] = jnp.zeros((TILE, width), jnp.float32)
        ext[place, TILE:right, : width - LANES] = ref[k, :, : width - LANES]
        ext[place, TILE:right, width - LANES :] = with_edge(
            ref[k, :, width - LANES :], rows, slab, used, n
        )
        ext[place, TILE - HALO : TILE] = jnp.where(left, 0.0, even[slab])
        ext[place, right : right + HALO] = jnp.where(left, even[slab], 0.0)


def box(ref, first, m):
    total = ref[first + m]
    for z in (m - 1, m + 1):
        if 0 <= z < 4:
            total = total + ref[first + z]
    rows, width = total.shape
    total = total + pltpu.roll(total, 1, 0) + pltpu.roll(total, rows - 1, 0)
    return total + pltpu.roll(total, 1, 1) + pltpu.roll(total, width - 1, 1)


def residual(ext, hh, qq, u, cu, e, m):
    base = ext.shape[0] - 4
    c, k = ext[base + m], e * 4 + m
    near_sum = box(u, e * 4, m) - u[k]
    weighted = box(cu, e * 4, m) - cu[k]
    return (qq[k] - u[k]) + hh[m] * (c * near_sum + weighted)


def second(ext, hh, qq, u1, cu1, u2, cu2, e, m):
    k = e * 4 + m
    p = (1.0 + KEEP1) * u1[k] + GAIN1 * residual(ext, hh, qq, u1, cu1, e, m)
    u2[k] = p
    cu2[k] = p * ext[ext.shape[0] - 4 + m]


def third(ext, hh, qq, u2, cu2, u3, cu3, mv, e, m):
    k = e * 4 + m
    step = GAIN0 * residual(ext, hh, qq, u2, cu2, e, m)
    p = u2[k] + step
    mv[k] = step
    u3[k] = p
    cu3[k] = p * ext[ext.shape[0] - 4 + m]


def fourth(ext, hh, qq, u3, cu3, mv, e, m):
    k = e * 4 + m
    return u3[k] + KEEP1 * mv[k] + GAIN1 * residual(ext, hh, qq, u3, cu3, e, m)


def start_sweeps(ext, hh, qq, u1, cu1):
    base = ext.shape[0] - 4
    for m in range(4):
        c = ext[base + m]
        diagonal = 0.5 * (26.0 * c + (box(ext, base, m) - c)) + mass_ratio * c
        inverse = jnp.where(c > 0.0, 1.0 / diagonal, 0.0)
        hh[m] = 0.5 * inverse
        for e in range(base // 4):
            q = ext[e * 4 + m] * inverse
            qq[e * 4 + m] = q
            u1[e * 4 + m] = GAIN0 * q
            cu1[e * 4 + m] = (GAIN0 * q) * c


def sweep_kernel(stride, _, odd, ext, trace, aux, hh, qq, u1, cu1, u2, cu2, u3, cu3, mv, u4):
    w = lax.axis_index("wide")
    inner = (w > 0) & (w < lax.axis_size("wide") - 1)
    excite = u4.shape[0]
    width = ext.shape[2]
    cells_x = ext.shape[1] - 2 * TILE
    right = TILE + cells_x
    left = lax.rem(w, 2) == 0
    for place, slab in enumerate(order(excite)):
        outer = jnp.where(inner, odd[slab], 0.0)
        for at, here in ((TILE - HALO, left), (right, ~left)):
            ext[place, at : at + HALO] = jnp.where(here, outer, ext[place, at : at + HALO])
    start_sweeps(ext, hh, qq, u1, cu1)
    for e in range(excite):
        for m in range(3):
            second(ext, hh, qq, u1, cu1, u2, cu2, e, m)
        for m in range(2):
            third(ext, hh, qq, u2, cu2, u3, cu3, mv, e, m)
        u4[e] = fourth(ext, hh, qq, u3, cu3, mv, e, 0)

    columns = 2 * excite
    r = lax.broadcasted_iota(jnp.int32, (trace.shape[1], width), 0)
    lane = lax.broadcasted_iota(jnp.int32, (trace.shape[1], width), 1)
    s = lax.div(r, columns)
    hit = lane == s * stride
    picked = jnp.zeros(trace.shape[1:], jnp.float32)
    for col in range(columns):
        e, late = col % excite, col >= excite
        match = hit & (lax.rem(r, columns) == col)
        if late:
            match = match & (s > 0)
        values = (u4[e, TILE:right] if late else u2[e * 4, TILE:right]).astype(jnp.bfloat16)
        picked = picked + nt(jnp.where(match, 1.0, 0.0).astype(jnp.bfloat16), values)
    for j in range(trace.shape[0]):
        trace[j] = picked.astype(jnp.bfloat16)
    aux[...] = jnp.zeros(aux.shape, jnp.float32)
    for k, source in enumerate([u4[e] for e in range(excite)] + [ext[4 * excite], hh[0]]):
        aux[k : k + 1] = source[TILE:right, 0:LANES].T[0:1]


def field_kernel(ext, pressure, near, hh, qq, u1, cu1, u2, cu2, u3, cu3, mv):
    v = lax.axis_index("vol")
    excite, _, cells_y, _ = pressure.shape
    right = ext.shape[1] - TILE
    start_sweeps(ext, hh, qq, u1, cu1)
    for e in range(excite):
        for m in range(4):
            second(ext, hh, qq, u1, cu1, u2, cu2, e, m)
        for m in range(3):
            third(ext, hh, qq, u2, cu2, u3, cu3, mv, e, m)
        for m in range(2):
            p = fourth(ext, hh, qq, u3, cu3, mv, e, m)
            pressure[e, inner_first(m, v)] = p[TILE:right].T[0:cells_y]
    near[...] = jnp.zeros(near.shape, jnp.float32)
    for m in range(2):
        for k, source in enumerate((ext[4 * excite + m, TILE:right], hh[m, TILE:right])):
            back = source.T
            for i, y in enumerate((0, 1, cells_y - 1)):
                row = 6 * k + 3 * m + i
                near[row : row + 1] = back[y : y + 1]


def product_kernel(blocks, operator, aux, out):
    count = blocks.shape[0]
    tile_rows = operator.shape[0]

    def pair(p, sums):
        both = jnp.concatenate([blocks[2 * p], blocks[2 * p + 1]], axis=1)
        sums = list(sums)
        for s in range(BY):
            start = pl.multiple_of(s * count * LANES + p * (2 * LANES), 2 * LANES)
            group = s // 4 * 16
            sums[s % 4] = sums[s % 4] + nt(both[group : group + 16], operator[:, pl.ds(start, 2 * LANES)])
        return tuple(sums)

    zero = jnp.zeros((16, tile_rows), jnp.float32)
    sums = lax.fori_loop(0, count // 2, pair, (zero,) * 4)
    r = lax.broadcasted_iota(jnp.int32, zero.shape, 0)
    total = zero
    for q in range(4):
        total = total + jnp.where((r >= 4 * q) & (r < 4 * q + 4), sums[q], 0.0)
    total = total[0:8] + total[8:16]
    total = total + pltpu.roll(total, 4, 0)
    r = lax.broadcasted_iota(jnp.int32, total.shape, 0)
    total = jnp.where(r < 4, total, pltpu.roll(aux[...], 4, 0))
    for j in range(out.shape[0]):
        out[j] = total


def couple_kernel(flat, mine, theirs, traction, fix, save):
    w, n = lax.axis_index("wide"), lax.axis_index("narrow")
    count = flat.shape[0] // 16
    excite = 2
    targets = mine.shape[0]

    def field(k, r):
        return flat[pl.ds(k * 8 + r, count, stride=16), :]

    lane = lax.broadcasted_iota(jnp.int32, (count, LANES), 1)
    sub = lax.broadcasted_iota(jnp.int32, (count, LANES), 0)

    def before(a):
        return pltpu.roll(a, 1, 1)

    def after(a):
        moved = pltpu.roll(a, LANES - 1, 1)
        following = jnp.where(sub == count - 1, 0.0, pltpu.roll(moved, count - 1, 0))
        return jnp.where(lane == LANES - 1, following, moved)

    own = (1.0 + KEEP1) * GAIN0 + GAIN1 - GAIN1 * GAIN0
    sides = []
    for k in range(2):
        c, h = field(k, 4 + excite), field(k, 5 + excite)
        rows = []
        for e in range(excite):
            t = field(0, e) + field(1, e)
            if k:
                t = pltpu.roll(t, LANES - targets, 1)
            t = jnp.where(lane < targets, t, 0.0)
            u = (2.0 * couple_gain) * h * t
            cu = c * u
            around, c_around = before(u) + after(u), before(cu) + after(cu)
            change = own * u + (GAIN0 * GAIN1) * h * (c * around + c_around)
            save[k, 0, e] = change
            save[k, 1, e] = around + u
            save[k, 2, e] = c_around + cu
            rows.append(field(k, 4 + e) + change)
        sides.append(rows)

    groups = count // 8
    total = jnp.zeros((16, targets), jnp.float32)
    r = lax.broadcasted_iota(jnp.int32, total.shape, 0)
    for g in range(groups):
        both = [
            jnp.concatenate([sides[k][e][8 * g : 8 * g + 8] for e in range(excite)], axis=0)
            for k in range(2)
        ]
        for ref, left in (
            (mine, jnp.where(n == 0, both[0], both[1])),
            (theirs, jnp.where(n == 0, both[1], both[0])),
        ):
            left = left.astype(jnp.bfloat16)
            for j in range(8):
                part = nt(left, ref[:, (8 * g + j) * LANES : (8 * g + j + 1) * LANES])
                total = total + jnp.where((r & 7) == j, part, 0.0)
    first = flat[pl.ds(pl.multiple_of(w * 16, 16), 8), :] + flat[pl.ds(pl.multiple_of(w * 16 + 8, 8), 8), :]
    first = jnp.where(n == 0, first, pltpu.roll(first, LANES - targets, 1))
    traction[...] = jnp.zeros(traction.shape, jnp.float32)
    for e in range(excite):
        traction[e : e + 1, 0:targets] = (
            jnp.sum(total[8 * e : 8 * e + 8], axis=0, keepdims=True)
            + first[2 + e : 3 + e, 0:targets]
        )

    fix[...] = jnp.zeros(fix.shape, jnp.float32)
    for e in range(excite):
        for i in range(3):
            row = 2 * i + e
            fix[row : row + 1] = save[n, i, e, pl.ds(w, 1), :]
        for i in range(1, 3):
            row = 4 + 2 * i + e
            fix[row : row + 1] = jnp.where(n == 0, save[1, i, e, pl.ds(w, 1), :], 0.0)


def mend_kernel(pressure, near, fix, out):
    v = lax.axis_index("vol")
    excite, _, cells_y, cells_x = pressure.shape
    r = lax.broadcasted_iota(jnp.int32, (8, cells_x), 0)
    out[...] = pressure[...]
    for e in range(excite):
        for m in range(2):
            li = v if m == 0 else 1 - v

            def change(i, a, b):
                c, h = near[3 * m + i : 3 * m + i + 1], near[6 + 3 * m + i : 7 + 3 * m + i]
                return (GAIN0 * GAIN1) * h * (c * fix[a + e : a + e + 1] + fix[b + e : b + e + 1])

            row0 = fix[e : e + 1] if m == 0 else change(0, 2, 4)
            delta = jnp.where(r == 0, row0, jnp.where(r == 1, change(1, 2, 4), 0.0))
            out[e, li, 0:8] = pressure[e, li, 0:8] + delta
            delta = jnp.where(r == 7, change(2, 6, 8), 0.0)
            out[e, li, cells_y - 8 : cells_y] = pressure[e, li, cells_y - 8 : cells_y] + delta


def local(forcing, material_ids, materials, boundary_operator):
    vols, wides, narrows = (lax.axis_size(a) for a in ("vol", "wide", "narrow"))
    v = lax.axis_index("vol")
    excite, layers, cells_y, cells_x = forcing.shape
    assert (vols, narrows, excite, layers, cells_x) == (2, 2, 2, 2, LANES)
    assert wides % 8 == 0 and wides & (wides - 1) == 0
    tile_rows = boundary_operator.shape[0]
    targets = tile_rows // narrows
    assert tile_rows == LANES and BY * 2 * excite == 64
    width = -(-(cells_y + 2 * HALO) // LANES) * LANES
    slabs = 4 * excite + 4
    f32, bf16 = jnp.float32, jnp.bfloat16
    everyone = ("vol", "wide", "narrow")
    vmem = pl.BlockSpec(memory_space=pltpu.VMEM)

    hbm = pl.BlockSpec(memory_space=pltpu.HBM)

    def call(kernel, shapes, specs, scratch=(), limit=4, **more):
        return pl.pallas_call(
            kernel,
            out_shape=[jax.ShapeDtypeStruct(*s) for s in shapes],
            in_specs=specs,
            out_specs=[vmem] * len(shapes),
            scratch_shapes=list(scratch),
            compiler_params=pltpu.CompilerParams(vmem_limit_bytes=limit * 2**20),
            **more,
        )

    def swap(x, axis):
        return lax.ppermute(x, axis, [(0, 1), (1, 0)])

    def number(a, b, c):
        return (a * wides + b) * narrows + c

    def in_hbm(x):
        return pltpu.with_memory_space_constraint(x, pltpu.HBM)

    dma = pltpu.SemaphoreType.DMA
    half = slabs // 2
    f_other, id_other = swap(forcing, "vol"), swap(material_ids, "vol")
    own, edge, spread, sent, mine = call(
        own_kernel,
        [
            ((half, cells_x, width), f32),
            ((half, HALO, cells_x), f32),
            ((materials.shape[0], LANES), f32),
        ]
        + [((targets, wides * LANES), bf16)] * 2,
        [hbm] * 4,
        [
            pltpu.VMEM(forcing.shape, f32),
            pltpu.VMEM(material_ids.shape, jnp.int32),
            pltpu.SMEM(materials.shape, f32),
            dma((5,)),
        ],
    )(in_hbm(materials), in_hbm(forcing), in_hbm(material_ids), in_hbm(boundary_operator))
    (edge,) = call(edge_kernel, [((slabs, HALO, cells_x), f32)], [vmem] * 4)(
        f_other, id_other, edge, spread
    )
    edge = swap(edge, "narrow")
    (other,) = call(other_kernel, [((half, cells_x, width), f32)], [vmem] * 3)(
        f_other, id_other, spread
    )
    used = cells_y - (width - LANES)
    even, odd, turned = call(
        functools.partial(side_kernel, used),
        [((slabs, HALO, width), f32)] * 2 + [((cells_x, LANES), f32)],
        [vmem] * 3,
    )(own, other, edge)
    even = lax.ppermute(even, "wide", [(i, i ^ 1) for i in range(wides)])
    odd_pairs = []
    for a in range(vols):
        for b in range(wides):
            for c in range(narrows):
                far = b + 1 if b % 2 else b - 1
                there = (far, c) if 0 <= far < wides else (b, 1 - c)
                odd_pairs.append((number(a, b, c), number(a, *there)))
    odd = lax.ppermute(odd, everyone, odd_pairs)
    rows = cells_x + 2 * TILE
    full = (rows, width)
    (ext,) = call(
        functools.partial(extend_kernel, used), [((slabs,) + full, f32)], [vmem] * 4
    )(own, other, turned, even)
    theirs = swap(sent, "narrow")
    many = pltpu.VMEM((4 * excite,) + full, f32)
    scratch = [pltpu.VMEM((4,) + full, f32)] + [many] * 8
    ext, trace, aux = call(
        functools.partial(sweep_kernel, cells_y // BY),
        [
            ((slabs,) + full, f32),
            ((wides, BY * 2 * excite, cells_x), bf16),
            ((8, cells_x), f32),
        ],
        [vmem] * 2,
        scratch + [pltpu.VMEM((excite,) + full, f32)],
        20,
        input_output_aliases={0: 0},
    )(ext, odd)

    def field(ext):
        shapes = [(forcing.shape, f32), ((16, cells_x), f32)]
        return call(field_kernel, shapes, [vmem], scratch, 20)(ext)

    def couple(ext, trace, aux, operator, theirs):
        blocks = lax.all_to_all(trace, "wide", 0, 0)
        pressure, near = field(ext)
        (sums,) = call(product_kernel, [((wides * narrows, 8, tile_rows), f32)], [vmem] * 3, (), 24)(
            blocks, operator, aux
        )
        blocks = lax.all_to_all(sums, ("wide", "narrow"), 0, 0)
        traction, fix = call(
            couple_kernel,
            [((8, LANES), f32), ((16, cells_x), f32)],
            [vmem] * 3,
            [pltpu.VMEM((2, 3, excite, wides, LANES), f32)],
        )(blocks.reshape(wides * narrows * 8, LANES), mine, theirs)
        return pressure, near, traction, fix

    def nothing(ext, *_):
        pressure, near = field(ext)
        return pressure, near, jnp.zeros((8, LANES), f32), jnp.zeros((16, cells_x), f32)

    pressure, near, traction, fix = lax.cond(
        v == vols - 1, couple, nothing, ext, trace, aux, boundary_operator, theirs
    )
    (pressure,) = call(mend_kernel, [(forcing.shape, f32)], [vmem] * 3)(pressure, near, fix)
    column = traction[0:2, :targets]
    lower = swap(column, "vol")
    column = jnp.where(v == vols - 1, column[1:2], lower[0:1])
    return pressure, column.reshape(targets, 1)


def solution(mesh):
    placed = (
        P(None, "vol", "narrow", "wide"),
        P("vol", "narrow", "wide"),
        P(),
        P("wide", "narrow"),
    )

    return jax.shard_map(
        local,
        mesh=mesh,
        in_specs=placed,
        out_specs=(P(None, "vol", "narrow", "wide"), P(("wide", "narrow"), "vol")),
        check_vma=False,
    )
```

```python
import functools

import jax
import jax.numpy as jnp
from jax import lax
from jax.experimental import pallas as pl
from jax.experimental.pallas import tpu as pltpu
from jax.sharding import PartitionSpec as P

BY = 16
HALO = 4
TILE = 8
LANES = 128

lower_edge = 0.25
upper_edge = 1.75
mass_ratio = 26.0
couple_gain = 40.0


def sweep_weights():
    middle = (upper_edge + lower_edge) / 2.0
    spread = (upper_edge - lower_edge) / 2.0
    center_ratio = middle / spread
    ratio_last = 1.0 / center_ratio
    ratio_next = 1.0 / (2.0 * center_ratio - ratio_last)
    return 1.0 / middle, ratio_next * ratio_last, 2.0 * ratio_next / spread


GAIN0, KEEP1, GAIN1 = sweep_weights()


def lookup(ids, table):
    found = jnp.zeros(ids.shape, jnp.float32)
    for number in range(table.shape[0]):
        found = jnp.where(ids == number, table[number], found)
    return found


def nt(a, b):
    return lax.dot_general(a, b, (((1,), (1,)), ((), ())), preferred_element_type=jnp.float32)


def inner_first(k, v):
    return v if k % 2 == 0 else 1 - v


def turn(block, out, slab):
    cells_y, cells_x = block.shape
    behind = jnp.zeros((out.shape[2] - cells_y, cells_x), jnp.float32)
    out[slab] = jnp.concatenate([block, behind], axis=0).T


def edge_rows(n, ref, *at):
    cells_y = ref.shape[-2]
    return jnp.where(
        n == 0, ref[*at, cells_y - HALO : cells_y, :], ref[*at, 0:HALO, :]
    )


def own_kernel(
    table, forcing, ids, operator, turned, edge, spread, sent, kept, f_in, id_in, table_in, sems
):
    v, n = lax.axis_index("vol"), lax.axis_index("narrow")
    targets, columns = sent.shape
    copies = [
        pltpu.make_async_copy(table, table_in, sems.at[0]),
        pltpu.make_async_copy(ids, id_in, sems.at[1]),
        pltpu.make_async_copy(forcing, f_in, sems.at[2]),
    ]
    for row, out in ((1 - n, sent), (n, kept)):
        rows = pl.ds(pl.multiple_of(row * targets, targets), targets)
        source = operator.at[rows, 0:columns]
        copies.append(pltpu.make_async_copy(source, out, sems.at[len(copies)]))
    for copy in copies:
        copy.start()
    excite = forcing.shape[0]
    copies[0].wait()
    for k in range(spread.shape[0]):
        spread[k : k + 1] = jnp.full((1, spread.shape[1]), table_in[k], jnp.float32)
    copies[1].wait()
    for m in range(2):
        li = inner_first(m, v)
        edge[2 * excite + m] = lookup(edge_rows(n, id_in, li), table_in)
        turn(lookup(id_in[li], table_in), turned, 2 * excite + m)
    copies[2].wait()
    for e in range(excite):
        for m in range(2):
            li = inner_first(m, v)
            edge[2 * e + m] = edge_rows(n, f_in, e, li)
            turn(f_in[e, li], turned, 2 * e + m)
    copies[3].wait()
    copies[4].wait()


def look_rows(ids, spread):
    found = jnp.zeros(ids.shape, jnp.float32)
    for number in range(spread.shape[0]):
        found = jnp.where(ids == number, spread[number : number + 1], found)
    return found


def edge_kernel(forcing, ids, own_edge, spread, edge):
    v, n = lax.axis_index("vol"), lax.axis_index("narrow")
    excite = forcing.shape[0]
    half = own_edge.shape[0]
    edge[0:half] = own_edge[...]
    for m in range(2):
        li = inner_first(m, v)
        edge[half + 2 * excite + m] = look_rows(edge_rows(n, ids, li), spread)
        for e in range(excite):
            edge[half + 2 * e + m] = edge_rows(n, forcing, e, li)


def other_kernel(forcing, ids, spread, turned):
    v = lax.axis_index("vol")
    excite = forcing.shape[0]
    for m in range(2):
        li = inner_first(m, v)
        turn(look_rows(ids[li], spread), turned, 2 * excite + m)
        for e in range(excite):
            turn(forcing[e, li], turned, 2 * e + m)


def turned_edge(got):
    slabs, halo, cells_x = got.shape
    rows = jnp.concatenate([got[k] for k in range(slabs)], axis=0)
    behind = jnp.zeros((LANES - slabs * halo, cells_x), jnp.float32)
    return jnp.concatenate([rows, behind], axis=0).T


def with_edge(last, rows, slab, used, n):
    base = jnp.where(n == 0, used, LANES - HALO)
    lane = lax.broadcasted_iota(jnp.int32, last.shape, 1)
    moved = pltpu.roll(rows, lax.rem(base - HALO * slab + LANES, LANES), 1)
    return jnp.where((lane >= base) & (lane < base + HALO), moved, last)


def side_kernel(used, own, other, got, even, odd, turned):
    w, n = lax.axis_index("wide"), lax.axis_index("narrow")
    half = own.shape[0]
    cells_x, width = own.shape[1], own.shape[2]
    rows = turned_edge(got)
    turned[...] = rows
    left = lax.rem(w, 2) == 0
    for slab in range(2 * half):
        ref, k = (own, slab) if slab < half else (other, slab - half)
        sides = []
        for at in (0, cells_x - TILE):
            last = with_edge(ref[k, at : at + TILE, width - LANES :], rows[at : at + TILE], slab, used, n)
            sides.append(jnp.concatenate([ref[k, at : at + TILE, : width - LANES], last], axis=1))
        first, last = sides[0][0:HALO], sides[1][TILE - HALO :]
        even[slab] = jnp.where(left, last, first)
        odd[slab] = jnp.where(left, first, last)


def order(excite):
    half = 2 * excite + 2
    kinds = list(range(excite)) + [excite]
    return [(0 if m < 2 else half) + 2 * k + m % 2 for k in kinds for m in range(4)]


def extend_kernel(used, own, other, turned, even, ext, saved, sems):
    n = lax.axis_index("narrow")
    half = own.shape[0]
    cells_x, width = own.shape[1], own.shape[2]
    right = TILE + cells_x
    left = lax.rem(lax.axis_index("wide"), 2) == 0
    rows = turned[...]
    copies = []
    for place, slab in enumerate(order((half - 2) // 2)):
        ref, k = (own, slab) if slab < half else (other, slab - half)
        ext[place, 0:TILE] = jnp.zeros((TILE, width), jnp.float32)
        ext[place, right : right + TILE] = jnp.zeros((TILE, width), jnp.float32)
        ext[place, TILE:right, : width - LANES] = ref[k, :, : width - LANES]
        ext[place, TILE:right, width - LANES :] = with_edge(
            ref[k, :, width - LANES :], rows, slab, used, n
        )
        ext[place, TILE - HALO : TILE] = jnp.where(left, 0.0, even[slab])
        ext[place, right : right + HALO] = jnp.where(left, even[slab], 0.0)
        copies.append(pltpu.make_async_copy(ext.at[place], saved.at[place], sems.at[place]))
        copies[place].start()
    for copy in copies:
        copy.wait()


def box(ref, first, m):
    total = ref[first + m]
    for z in (m - 1, m + 1):
        if 0 <= z < 4:
            total = total + ref[first + z]
    rows, width = total.shape
    total = total + pltpu.roll(total, 1, 0) + pltpu.roll(total, rows - 1, 0)
    return total + pltpu.roll(total, 1, 1) + pltpu.roll(total, width - 1, 1)


def residual(ext, hh, qq, u, cu, e, m):
    base = ext.shape[0] - 4
    c, k = ext[base + m], e * 4 + m
    near_sum = box(u, e * 4, m) - u[k]
    weighted = box(cu, e * 4, m) - cu[k]
    return (qq[k] - u[k]) + hh[m] * (c * near_sum + weighted)


def second(ext, hh, qq, u1, cu1, u2, cu2, e, m):
    k = e * 4 + m
    p = (1.0 + KEEP1) * u1[k] + GAIN1 * residual(ext, hh, qq, u1, cu1, e, m)
    u2[k] = p
    cu2[k] = p * ext[ext.shape[0] - 4 + m]


def third(ext, hh, qq, u2, cu2, u3, cu3, mv, e, m):
    k = e * 4 + m
    step = GAIN0 * residual(ext, hh, qq, u2, cu2, e, m)
    p = u2[k] + step
    mv[k] = step
    u3[k] = p
    cu3[k] = p * ext[ext.shape[0] - 4 + m]


def fourth(ext, hh, qq, u3, cu3, mv, e, m):
    k = e * 4 + m
    return u3[k] + KEEP1 * mv[k] + GAIN1 * residual(ext, hh, qq, u3, cu3, e, m)


def start_sweeps(ext, hh, qq, u1, cu1):
    base = ext.shape[0] - 4
    for m in range(4):
        c = ext[base + m]
        diagonal = 0.5 * (26.0 * c + (box(ext, base, m) - c)) + mass_ratio * c
        inverse = jnp.where(c > 0.0, 1.0 / diagonal, 0.0)
        hh[m] = 0.5 * inverse
        for e in range(base // 4):
            q = ext[e * 4 + m] * inverse
            qq[e * 4 + m] = q
            u1[e * 4 + m] = GAIN0 * q
            cu1[e * 4 + m] = (GAIN0 * q) * c


def sweep_kernel(
    stride, _, __, odd, ext, saved, trace, aux, hh, qq, u1, cu1, u2, cu2, u3, cu3, mv, u4, sems
):
    w = lax.axis_index("wide")
    inner = (w > 0) & (w < lax.axis_size("wide") - 1)
    excite = u4.shape[0]
    width = ext.shape[2]
    cells_x = ext.shape[1] - 2 * TILE
    right = TILE + cells_x
    left = lax.rem(w, 2) == 0
    for place, slab in enumerate(order(excite)):
        outer = jnp.where(inner, odd[slab], 0.0)
        for at, here in ((TILE - HALO, left), (right, ~left)):
            ext[place, at : at + HALO] = jnp.where(here, outer, ext[place, at : at + HALO])
    copies = []
    for k, at in enumerate((0, right)):
        edge = ext.at[:, at : at + TILE], saved.at[:, at : at + TILE]
        copies.append(pltpu.make_async_copy(*edge, sems.at[k]))
        copies[k].start()
    start_sweeps(ext, hh, qq, u1, cu1)
    for e in range(excite):
        for m in range(3):
            second(ext, hh, qq, u1, cu1, u2, cu2, e, m)
        for m in range(2):
            third(ext, hh, qq, u2, cu2, u3, cu3, mv, e, m)
        u4[e] = fourth(ext, hh, qq, u3, cu3, mv, e, 0)

    columns = 2 * excite
    r = lax.broadcasted_iota(jnp.int32, (trace.shape[1], width), 0)
    lane = lax.broadcasted_iota(jnp.int32, (trace.shape[1], width), 1)
    s = lax.div(r, columns)
    hit = lane == s * stride
    picked = jnp.zeros(trace.shape[1:], jnp.float32)
    for col in range(columns):
        e, late = col % excite, col >= excite
        match = hit & (lax.rem(r, columns) == col)
        if late:
            match = match & (s > 0)
        values = (u4[e, TILE:right] if late else u2[e * 4, TILE:right]).astype(jnp.bfloat16)
        picked = picked + nt(jnp.where(match, 1.0, 0.0).astype(jnp.bfloat16), values)
    for j in range(trace.shape[0]):
        trace[j] = picked.astype(jnp.bfloat16)
    aux[...] = jnp.zeros(aux.shape, jnp.float32)
    for k, source in enumerate([u4[e] for e in range(excite)] + [ext[4 * excite], hh[0]]):
        aux[k : k + 1] = source[TILE:right, 0:LANES].T[0:1]
    for copy in copies:
        copy.wait()


def field_kernel(ext, pressure, near, hh, qq, u1, cu1, u2, cu2, u3, cu3, mv):
    v = lax.axis_index("vol")
    excite, _, cells_y, _ = pressure.shape
    right = ext.shape[1] - TILE
    start_sweeps(ext, hh, qq, u1, cu1)
    for e in range(excite):
        for m in range(4):
            second(ext, hh, qq, u1, cu1, u2, cu2, e, m)
        for m in range(3):
            third(ext, hh, qq, u2, cu2, u3, cu3, mv, e, m)
        for m in range(2):
            p = fourth(ext, hh, qq, u3, cu3, mv, e, m)
            pressure[e, inner_first(m, v)] = p[TILE:right].T[0:cells_y]
    near[...] = jnp.zeros(near.shape, jnp.float32)
    for m in range(2):
        for k, source in enumerate((ext[4 * excite + m, TILE:right], hh[m, TILE:right])):
            back = source.T
            for i, y in enumerate((0, 1, cells_y - 1)):
                row = 6 * k + 3 * m + i
                near[row : row + 1] = back[y : y + 1]


def product_kernel(blocks, operator, aux, out):
    count = blocks.shape[0]
    tile_rows = operator.shape[0]

    def pairs(first, sums):
        sums = list(sums)
        for p in range(4):
            p = first * 4 + p
            both = jnp.concatenate([blocks[2 * p], blocks[2 * p + 1]], axis=1)
            for s in range(BY):
                start = s * count * LANES + p * (2 * LANES)
                if not isinstance(start, int):
                    start = pl.multiple_of(start, 2 * LANES)
                group = s // 4 * 16
                sums[s % 4] = sums[s % 4] + nt(
                    both[group : group + 16], operator[:, pl.ds(start, 2 * LANES)]
                )
        return tuple(sums)

    zero = jnp.zeros((16, tile_rows), jnp.float32)
    sums = (zero,) * 4
    if count == 8:
        sums = pairs(0, sums)
    else:
        sums = lax.fori_loop(0, count // 8, pairs, sums)
    r = lax.broadcasted_iota(jnp.int32, zero.shape, 0)
    total = zero
    for q in range(4):
        total = total + jnp.where((r >= 4 * q) & (r < 4 * q + 4), sums[q], 0.0)
    total = total[0:8] + total[8:16]
    total = total + pltpu.roll(total, 4, 0)
    r = lax.broadcasted_iota(jnp.int32, total.shape, 0)
    total = jnp.where(r < 4, total, pltpu.roll(aux[...], 4, 0))
    for j in range(out.shape[0]):
        out[j] = total


def couple_kernel(flat, mine, theirs, traction, fix, save):
    w, n = lax.axis_index("wide"), lax.axis_index("narrow")
    count = flat.shape[0] // 16
    excite = 2
    targets = mine.shape[0]

    def field(k, r):
        return flat[pl.ds(k * 8 + r, count, stride=16), :]

    lane = lax.broadcasted_iota(jnp.int32, (count, LANES), 1)
    sub = lax.broadcasted_iota(jnp.int32, (count, LANES), 0)

    def before(a):
        return pltpu.roll(a, 1, 1)

    def after(a):
        moved = pltpu.roll(a, LANES - 1, 1)
        following = jnp.where(sub == count - 1, 0.0, pltpu.roll(moved, count - 1, 0))
        return jnp.where(lane == LANES - 1, following, moved)

    own = (1.0 + KEEP1) * GAIN0 + GAIN1 - GAIN1 * GAIN0
    sides = []
    for k in range(2):
        c, h = field(k, 4 + excite), field(k, 5 + excite)
        rows = []
        for e in range(excite):
            t = field(0, e) + field(1, e)
            if k:
                t = pltpu.roll(t, LANES - targets, 1)
            t = jnp.where(lane < targets, t, 0.0)
            u = (2.0 * couple_gain) * h * t
            cu = c * u
            around, c_around = before(u) + after(u), before(cu) + after(cu)
            change = own * u + (GAIN0 * GAIN1) * h * (c * around + c_around)
            save[k, 0, e] = change
            save[k, 1, e] = around + u
            save[k, 2, e] = c_around + cu
            rows.append(field(k, 4 + e) + change)
        sides.append(rows)

    groups = count // 8
    total = jnp.zeros((16, targets), jnp.float32)
    r = lax.broadcasted_iota(jnp.int32, total.shape, 0)
    for g in range(groups):
        both = [
            jnp.concatenate([sides[k][e][8 * g : 8 * g + 8] for e in range(excite)], axis=0)
            for k in range(2)
        ]
        for ref, left in (
            (mine, jnp.where(n == 0, both[0], both[1])),
            (theirs, jnp.where(n == 0, both[1], both[0])),
        ):
            left = left.astype(jnp.bfloat16)
            for j in range(8):
                part = nt(left, ref[:, (8 * g + j) * LANES : (8 * g + j + 1) * LANES])
                total = total + jnp.where((r & 7) == j, part, 0.0)
    first = flat[pl.ds(pl.multiple_of(w * 16, 16), 8), :] + flat[pl.ds(pl.multiple_of(w * 16 + 8, 8), 8), :]
    first = jnp.where(n == 0, first, pltpu.roll(first, LANES - targets, 1))
    traction[...] = jnp.zeros(traction.shape, jnp.float32)
    for e in range(excite):
        traction[e : e + 1, 0:targets] = (
            jnp.sum(total[8 * e : 8 * e + 8], axis=0, keepdims=True)
            + first[2 + e : 3 + e, 0:targets]
        )

    fix[...] = jnp.zeros(fix.shape, jnp.float32)
    for e in range(excite):
        for i in range(3):
            row = 2 * i + e
            fix[row : row + 1] = save[n, i, e, pl.ds(w, 1), :]
        for i in range(1, 3):
            row = 4 + 2 * i + e
            fix[row : row + 1] = jnp.where(n == 0, save[1, i, e, pl.ds(w, 1), :], 0.0)


def mend_kernel(pressure, near, fix, out):
    v = lax.axis_index("vol")
    excite, _, cells_y, cells_x = pressure.shape
    r = lax.broadcasted_iota(jnp.int32, (8, cells_x), 0)
    out[...] = pressure[...]
    for e in range(excite):
        for m in range(2):
            li = v if m == 0 else 1 - v

            def change(i, a, b):
                c, h = near[3 * m + i : 3 * m + i + 1], near[6 + 3 * m + i : 7 + 3 * m + i]
                return (GAIN0 * GAIN1) * h * (c * fix[a + e : a + e + 1] + fix[b + e : b + e + 1])

            row0 = fix[e : e + 1] if m == 0 else change(0, 2, 4)
            delta = jnp.where(r == 0, row0, jnp.where(r == 1, change(1, 2, 4), 0.0))
            out[e, li, 0:8] = pressure[e, li, 0:8] + delta
            delta = jnp.where(r == 7, change(2, 6, 8), 0.0)
            out[e, li, cells_y - 8 : cells_y] = pressure[e, li, cells_y - 8 : cells_y] + delta


def local(forcing, material_ids, materials, boundary_operator):
    vols, wides, narrows = (lax.axis_size(a) for a in ("vol", "wide", "narrow"))
    v = lax.axis_index("vol")
    excite, layers, cells_y, cells_x = forcing.shape
    assert (vols, narrows, excite, layers, cells_x) == (2, 2, 2, 2, LANES)
    assert wides % 8 == 0 and wides & (wides - 1) == 0
    tile_rows = boundary_operator.shape[0]
    targets = tile_rows // narrows
    assert tile_rows == LANES and BY * 2 * excite == 64
    width = -(-(cells_y + 2 * HALO) // LANES) * LANES
    slabs = 4 * excite + 4
    f32, bf16 = jnp.float32, jnp.bfloat16
    everyone = ("vol", "wide", "narrow")
    vmem = pl.BlockSpec(memory_space=pltpu.VMEM)

    hbm = pl.BlockSpec(memory_space=pltpu.HBM)

    def call(kernel, shapes, specs, scratch=(), limit=4, outs=None, **more):
        return pl.pallas_call(
            kernel,
            out_shape=[jax.ShapeDtypeStruct(*s) if isinstance(s, tuple) else s for s in shapes],
            in_specs=specs,
            out_specs=outs or [vmem] * len(shapes),
            scratch_shapes=list(scratch),
            compiler_params=pltpu.CompilerParams(vmem_limit_bytes=limit * 2**20),
            **more,
        )

    def swap(x, axis):
        return lax.ppermute(x, axis, [(0, 1), (1, 0)])

    def number(a, b, c):
        return (a * wides + b) * narrows + c

    def in_hbm(x):
        return pltpu.with_memory_space_constraint(x, pltpu.HBM)

    dma = pltpu.SemaphoreType.DMA
    half = slabs // 2
    f_other, id_other = swap(forcing, "vol"), swap(material_ids, "vol")
    own, edge, spread, sent, mine = call(
        own_kernel,
        [
            ((half, cells_x, width), f32),
            ((half, HALO, cells_x), f32),
            ((materials.shape[0], LANES), f32),
        ]
        + [((targets, wides * LANES), bf16)] * 2,
        [hbm] * 4,
        [
            pltpu.VMEM(forcing.shape, f32),
            pltpu.VMEM(material_ids.shape, jnp.int32),
            pltpu.SMEM(materials.shape, f32),
            dma((5,)),
        ],
    )(in_hbm(materials), in_hbm(forcing), in_hbm(material_ids), in_hbm(boundary_operator))
    (edge,) = call(edge_kernel, [((slabs, HALO, cells_x), f32)], [vmem] * 4)(
        f_other, id_other, edge, spread
    )
    edge = swap(edge, "narrow")
    (other,) = call(other_kernel, [((half, cells_x, width), f32)], [vmem] * 3)(
        f_other, id_other, spread
    )
    used = cells_y - (width - LANES)
    even, odd, turned = call(
        functools.partial(side_kernel, used),
        [((slabs, HALO, width), f32)] * 2 + [((cells_x, LANES), f32)],
        [vmem] * 3,
    )(own, other, edge)
    even = lax.ppermute(even, "wide", [(i, i ^ 1) for i in range(wides)])
    odd_pairs = []
    for a in range(vols):
        for b in range(wides):
            for c in range(narrows):
                far = b + 1 if b % 2 else b - 1
                there = (far, c) if 0 <= far < wides else (b, 1 - c)
                odd_pairs.append((number(a, b, c), number(a, *there)))
    odd = lax.ppermute(odd, everyone, odd_pairs)
    rows = cells_x + 2 * TILE
    full = (rows, width)
    ext, saved = call(
        functools.partial(extend_kernel, used),
        [((slabs,) + full, f32), pltpu.HBM((slabs,) + full, f32)],
        [vmem] * 4,
        [dma((slabs,))],
        outs=[vmem, hbm],
    )(own, other, turned, even)
    theirs = swap(sent, "narrow")
    many = pltpu.VMEM((4 * excite,) + full, f32)
    scratch = [pltpu.VMEM((4,) + full, f32)] + [many] * 8
    _, ext, trace, aux = call(
        functools.partial(sweep_kernel, cells_y // BY),
        [
            ((slabs,) + full, f32),
            pltpu.HBM((slabs,) + full, f32),
            ((wides, BY * 2 * excite, cells_x), bf16),
            ((8, cells_x), f32),
        ],
        [vmem, hbm, vmem],
        scratch + [pltpu.VMEM((excite,) + full, f32), dma((2,))],
        20,
        outs=[vmem, hbm, vmem, vmem],
        input_output_aliases={0: 0, 1: 1},
    )(ext, saved, odd)

    def field(ext):
        shapes = [(forcing.shape, f32), ((16, cells_x), f32)]
        return call(field_kernel, shapes, [vmem], scratch, 20)(ext)

    def couple(ext, trace, aux, operator, theirs):
        blocks = lax.all_to_all(trace, "wide", 0, 0)
        pressure, near = field(ext)
        (sums,) = call(product_kernel, [((wides * narrows, 8, tile_rows), f32)], [vmem] * 3, (), 24)(
            blocks, operator, aux
        )
        blocks = lax.all_to_all(sums, ("wide", "narrow"), 0, 0)
        traction, fix = call(
            couple_kernel,
            [((8, LANES), f32), ((16, cells_x), f32)],
            [vmem] * 3,
            [pltpu.VMEM((2, 3, excite, wides, LANES), f32)],
        )(blocks.reshape(wides * narrows * 8, LANES), mine, theirs)
        return pressure, near, traction, fix

    def nothing(ext, *_):
        pressure, near = field(ext)
        return pressure, near, jnp.zeros((8, LANES), f32), jnp.zeros((16, cells_x), f32)

    pressure, near, traction, fix = lax.cond(
        v == vols - 1, couple, nothing, ext, trace, aux, boundary_operator, theirs
    )
    (pressure,) = call(mend_kernel, [(forcing.shape, f32)], [vmem] * 3)(pressure, near, fix)
    column = traction[0:2, :targets]
    lower = swap(column, "vol")
    column = jnp.where(v == vols - 1, column[1:2], lower[0:1])
    return pressure, column.reshape(targets, 1)


def solution(mesh):
    placed = (
        P(None, "vol", "narrow", "wide"),
        P("vol", "narrow", "wide"),
        P(),
        P("wide", "narrow"),
    )

    return jax.shard_map(
        local,
        mesh=mesh,
        in_specs=placed,
        out_specs=(P(None, "vol", "narrow", "wide"), P(("wide", "narrow"), "vol")),
        check_vma=False,
    )
```

```python
import functools

import jax
import jax.numpy as jnp
from jax import lax
from jax.experimental import pallas as pl
from jax.experimental.pallas import tpu as pltpu
from jax.sharding import PartitionSpec as P

BY = 16
HALO = 4
TILE = 8
LANES = 128

lower_edge = 0.25
upper_edge = 1.75
mass_ratio = 26.0
couple_gain = 40.0


def sweep_weights():
    middle = (upper_edge + lower_edge) / 2.0
    spread = (upper_edge - lower_edge) / 2.0
    center_ratio = middle / spread
    ratio_last = 1.0 / center_ratio
    ratio_next = 1.0 / (2.0 * center_ratio - ratio_last)
    return 1.0 / middle, ratio_next * ratio_last, 2.0 * ratio_next / spread


GAIN0, KEEP1, GAIN1 = sweep_weights()


def lookup(ids, table):
    found = jnp.zeros(ids.shape, jnp.float32)
    for number in range(table.shape[0]):
        found = jnp.where(ids == number, table[number], found)
    return found


def nt(a, b):
    return lax.dot_general(a, b, (((1,), (1,)), ((), ())), preferred_element_type=jnp.float32)


def inner_first(k, v):
    return v if k % 2 == 0 else 1 - v


def turn(block, out, slab):
    cells_y, cells_x = block.shape
    behind = jnp.zeros((out.shape[2] - cells_y, cells_x), jnp.float32)
    out[slab] = jnp.concatenate([block, behind], axis=0).T


def edge_rows(n, ref, *at):
    cells_y = ref.shape[-2]
    return jnp.where(
        n == 0, ref[*at, cells_y - HALO : cells_y, :], ref[*at, 0:HALO, :]
    )


def own_kernel(
    table, forcing, ids, operator, turned, edge, spread, sent, kept, f_in, id_in, table_in, sems
):
    v, n = lax.axis_index("vol"), lax.axis_index("narrow")
    targets, columns = sent.shape
    copies = [
        pltpu.make_async_copy(table, table_in, sems.at[0]),
        pltpu.make_async_copy(ids, id_in, sems.at[1]),
        pltpu.make_async_copy(forcing, f_in, sems.at[2]),
    ]
    for row, out in ((1 - n, sent), (n, kept)):
        rows = pl.ds(pl.multiple_of(row * targets, targets), targets)
        source = operator.at[rows, 0:columns]
        copies.append(pltpu.make_async_copy(source, out, sems.at[len(copies)]))
    for copy in copies:
        copy.start()
    excite = forcing.shape[0]
    copies[0].wait()
    for k in range(spread.shape[0]):
        spread[k : k + 1] = jnp.full((1, spread.shape[1]), table_in[k], jnp.float32)
    copies[1].wait()
    for m in range(2):
        li = inner_first(m, v)
        edge[2 * excite + m] = lookup(edge_rows(n, id_in, li), table_in)
        turn(lookup(id_in[li], table_in), turned, 2 * excite + m)
    copies[2].wait()
    for e in range(excite):
        for m in range(2):
            li = inner_first(m, v)
            edge[2 * e + m] = edge_rows(n, f_in, e, li)
            turn(f_in[e, li], turned, 2 * e + m)
    copies[3].wait()
    copies[4].wait()


def look_rows(ids, spread):
    found = jnp.zeros(ids.shape, jnp.float32)
    for number in range(spread.shape[0]):
        found = jnp.where(ids == number, spread[number : number + 1], found)
    return found


def edge_kernel(forcing, ids, own_edge, spread, edge):
    v, n = lax.axis_index("vol"), lax.axis_index("narrow")
    excite = forcing.shape[0]
    half = own_edge.shape[0]
    edge[0:half] = own_edge[...]
    for m in range(2):
        li = inner_first(m, v)
        edge[half + 2 * excite + m] = look_rows(edge_rows(n, ids, li), spread)
        for e in range(excite):
            edge[half + 2 * e + m] = edge_rows(n, forcing, e, li)


def other_kernel(forcing, ids, spread, turned):
    v = lax.axis_index("vol")
    excite = forcing.shape[0]
    for m in range(2):
        li = inner_first(m, v)
        turn(look_rows(ids[li], spread), turned, 2 * excite + m)
        for e in range(excite):
            turn(forcing[e, li], turned, 2 * e + m)


def turned_edge(got):
    slabs, halo, cells_x = got.shape
    rows = jnp.concatenate([got[k] for k in range(slabs)], axis=0)
    behind = jnp.zeros((LANES - slabs * halo, cells_x), jnp.float32)
    return jnp.concatenate([rows, behind], axis=0).T


def with_edge(last, rows, slab, used, n):
    base = jnp.where(n == 0, used, LANES - HALO)
    lane = lax.broadcasted_iota(jnp.int32, last.shape, 1)
    moved = pltpu.roll(rows, lax.rem(base - HALO * slab + LANES, LANES), 1)
    return jnp.where((lane >= base) & (lane < base + HALO), moved, last)


def side_kernel(used, own, other, got, even, odd, turned):
    w, n = lax.axis_index("wide"), lax.axis_index("narrow")
    half = own.shape[0]
    cells_x, width = own.shape[1], own.shape[2]
    rows = turned_edge(got)
    turned[...] = rows
    left = lax.rem(w, 2) == 0
    for slab in range(2 * half):
        ref, k = (own, slab) if slab < half else (other, slab - half)
        sides = []
        for at in (0, cells_x - TILE):
            last = with_edge(ref[k, at : at + TILE, width - LANES :], rows[at : at + TILE], slab, used, n)
            sides.append(jnp.concatenate([ref[k, at : at + TILE, : width - LANES], last], axis=1))
        first, last = sides[0][0:HALO], sides[1][TILE - HALO :]
        even[slab] = jnp.where(left, last, first)
        odd[slab] = jnp.where(left, first, last)


def order(excite):
    half = 2 * excite + 2
    kinds = list(range(excite)) + [excite]
    return [(0 if m < 2 else half) + 2 * k + m % 2 for k in kinds for m in range(4)]


def extend_kernel(used, own, other, turned, ext, saved, sems):
    n = lax.axis_index("narrow")
    half = own.shape[0]
    cells_x, width = own.shape[1], own.shape[2]
    right = TILE + cells_x
    rows = turned[...]
    copies = []
    for place, slab in enumerate(order((half - 2) // 2)):
        ref, k = (own, slab) if slab < half else (other, slab - half)
        ext[place, 0:TILE] = jnp.zeros((TILE, width), jnp.float32)
        ext[place, right : right + TILE] = jnp.zeros((TILE, width), jnp.float32)
        ext[place, TILE:right, : width - LANES] = ref[k, :, : width - LANES]
        ext[place, TILE:right, width - LANES :] = with_edge(
            ref[k, :, width - LANES :], rows, slab, used, n
        )
        copies.append(pltpu.make_async_copy(ext.at[place], saved.at[place], sems.at[place]))
        copies[place].start()
    for copy in copies:
        copy.wait()


def box(ref, first, m):
    total = ref[first + m]
    for z in (m - 1, m + 1):
        if 0 <= z < 4:
            total = total + ref[first + z]
    rows, width = total.shape
    total = total + pltpu.roll(total, 1, 0) + pltpu.roll(total, rows - 1, 0)
    return total + pltpu.roll(total, 1, 1) + pltpu.roll(total, width - 1, 1)


def drawn(ext, hh, u, cu, e, m):
    base = ext.shape[0] - 4
    c, k = ext[base + m], e * 4 + m
    near_sum = box(u, e * 4, m) - u[k]
    weighted = box(cu, e * 4, m) - cu[k]
    return hh[m] * (c * near_sum + weighted)


def residual(ext, hh, qq, u, cu, e, m):
    k = e * 4 + m
    return (qq[k] - u[k]) + drawn(ext, hh, u, cu, e, m)


def second(ext, hh, u1, cu1, u2, cu2, e, m):
    k = e * 4 + m
    p = (1.0 + KEEP1 + GAIN1 / GAIN0 - GAIN1) * u1[k] + GAIN1 * drawn(ext, hh, u1, cu1, e, m)
    u2[k] = p
    cu2[k] = p * ext[ext.shape[0] - 4 + m]


def third(ext, hh, qq, u2, cu2, u3, cu3, mv, e, m):
    k = e * 4 + m
    step = GAIN0 * residual(ext, hh, qq, u2, cu2, e, m)
    p = u2[k] + step
    mv[k] = step
    u3[k] = p
    cu3[k] = p * ext[ext.shape[0] - 4 + m]


def fourth(ext, hh, qq, u3, cu3, mv, e, m):
    k = e * 4 + m
    return u3[k] + KEEP1 * mv[k] + GAIN1 * residual(ext, hh, qq, u3, cu3, e, m)


def start_sweeps(ext, hh, qq, u1, cu1):
    base = ext.shape[0] - 4
    for m in range(4):
        c = ext[base + m]
        diagonal = 0.5 * (26.0 * c + (box(ext, base, m) - c)) + mass_ratio * c
        inverse = jnp.where(c > 0.0, 1.0 / diagonal, 0.0)
        hh[m] = 0.5 * inverse
        for e in range(base // 4):
            q = ext[e * 4 + m] * inverse
            qq[e * 4 + m] = q
            u1[e * 4 + m] = GAIN0 * q
            cu1[e * 4 + m] = (GAIN0 * q) * c


def merge_sides(even, odd, ext):
    w = lax.axis_index("wide")
    inner = (w > 0) & (w < lax.axis_size("wide") - 1)
    left = lax.rem(w, 2) == 0
    right = ext.shape[1] - TILE
    for place, slab in enumerate(order(ext.shape[0] // 4 - 1)):
        outer = jnp.where(inner, odd[slab], 0.0)
        ext[place, TILE - HALO : TILE] = jnp.where(left, outer, even[slab])
        ext[place, right : right + HALO] = jnp.where(left, even[slab], outer)


def sweep_kernel(
    stride, _, __, even, odd, ext, saved, trace, aux, hh, qq, u1, cu1, u2, cu2, u3, cu3, mv, u4, sems
):
    excite = u4.shape[0]
    width = ext.shape[2]
    cells_x = ext.shape[1] - 2 * TILE
    right = TILE + cells_x
    merge_sides(even, odd, ext)
    copies = []
    for k, at in enumerate((0, right)):
        edge = ext.at[:, at : at + TILE], saved.at[:, at : at + TILE]
        copies.append(pltpu.make_async_copy(*edge, sems.at[k]))
        copies[k].start()
    start_sweeps(ext, hh, qq, u1, cu1)
    for e in range(excite):
        for m in range(3):
            second(ext, hh, u1, cu1, u2, cu2, e, m)
        for m in range(2):
            third(ext, hh, qq, u2, cu2, u3, cu3, mv, e, m)
        u4[e] = fourth(ext, hh, qq, u3, cu3, mv, e, 0)

    columns = 2 * excite
    r = lax.broadcasted_iota(jnp.int32, (trace.shape[1], width), 0)
    lane = lax.broadcasted_iota(jnp.int32, (trace.shape[1], width), 1)
    s = lax.div(r, columns)
    hit = lane == s * stride
    picked = jnp.zeros(trace.shape[1:], jnp.float32)
    for col in range(columns):
        e, late = col % excite, col >= excite
        match = hit & (lax.rem(r, columns) == col)
        if late:
            match = match & (s > 0)
        values = (u4[e, TILE:right] if late else u2[e * 4, TILE:right]).astype(jnp.bfloat16)
        picked = picked + nt(jnp.where(match, 1.0, 0.0).astype(jnp.bfloat16), values)
    for j in range(trace.shape[0]):
        trace[j] = picked.astype(jnp.bfloat16)
    aux[...] = jnp.zeros(aux.shape, jnp.float32)
    for k, source in enumerate([u4[e] for e in range(excite)] + [ext[4 * excite], hh[0]]):
        aux[k : k + 1] = source[TILE:right, 0:LANES].T[0:1]
    for copy in copies:
        copy.wait()


def field_kernel(ext, pressure, near, hh, qq, u1, cu1, u2, cu2, u3, cu3, mv):
    v = lax.axis_index("vol")
    excite, _, cells_y, _ = pressure.shape
    right = ext.shape[1] - TILE
    start_sweeps(ext, hh, qq, u1, cu1)
    for e in range(excite):
        for m in range(4):
            second(ext, hh, u1, cu1, u2, cu2, e, m)
        for m in range(3):
            third(ext, hh, qq, u2, cu2, u3, cu3, mv, e, m)
        for m in range(2):
            p = fourth(ext, hh, qq, u3, cu3, mv, e, m)
            pressure[e, inner_first(m, v)] = p[TILE:right].T[0:cells_y]
    near[...] = jnp.zeros(near.shape, jnp.float32)
    for m in range(2):
        for k, source in enumerate((ext[4 * excite + m, TILE:right], hh[m, TILE:right])):
            back = source.T
            for i, y in enumerate((0, 1, cells_y - 1)):
                row = 6 * k + 3 * m + i
                near[row : row + 1] = back[y : y + 1]


def lower_kernel(_, even, odd, ext, pressure, near, *scratch):
    merge_sides(even, odd, ext)
    field_kernel(ext, pressure, near, *scratch)


def product_kernel(blocks, operator, aux, out):
    count = blocks.shape[0]
    tile_rows = operator.shape[0]

    def pairs(first, sums):
        sums = list(sums)
        for p in range(4):
            p = first * 4 + p
            both = jnp.concatenate([blocks[2 * p], blocks[2 * p + 1]], axis=1)
            for s in range(BY):
                start = s * count * LANES + p * (2 * LANES)
                if not isinstance(start, int):
                    start = pl.multiple_of(start, 2 * LANES)
                group = s // 4 * 16
                sums[s % 4] = sums[s % 4] + nt(
                    both[group : group + 16], operator[:, pl.ds(start, 2 * LANES)]
                )
        return tuple(sums)

    zero = jnp.zeros((16, tile_rows), jnp.float32)
    sums = (zero,) * 4
    if count == 8:
        sums = pairs(0, sums)
    else:
        sums = lax.fori_loop(0, count // 8, pairs, sums)
    r = lax.broadcasted_iota(jnp.int32, zero.shape, 0)
    total = zero
    for q in range(4):
        total = total + jnp.where((r >= 4 * q) & (r < 4 * q + 4), sums[q], 0.0)
    total = total[0:8] + total[8:16]
    total = total + pltpu.roll(total, 4, 0)
    r = lax.broadcasted_iota(jnp.int32, total.shape, 0)
    total = jnp.where(r < 4, total, pltpu.roll(aux[...], 4, 0))
    for j in range(out.shape[0]):
        out[j] = total


def couple_kernel(flat, mine, theirs, traction, fix, save):
    w, n = lax.axis_index("wide"), lax.axis_index("narrow")
    count = flat.shape[0] // 16
    excite = 2
    targets = mine.shape[0]

    def field(k, r):
        return flat[pl.ds(k * 8 + r, count, stride=16), :]

    lane = lax.broadcasted_iota(jnp.int32, (count, LANES), 1)
    sub = lax.broadcasted_iota(jnp.int32, (count, LANES), 0)

    def before(a):
        return pltpu.roll(a, 1, 1)

    def after(a):
        moved = pltpu.roll(a, LANES - 1, 1)
        following = jnp.where(sub == count - 1, 0.0, pltpu.roll(moved, count - 1, 0))
        return jnp.where(lane == LANES - 1, following, moved)

    own = (1.0 + KEEP1) * GAIN0 + GAIN1 - GAIN1 * GAIN0
    sides = []
    for k in range(2):
        c, h = field(k, 4 + excite), field(k, 5 + excite)
        rows = []
        for e in range(excite):
            t = field(0, e) + field(1, e)
            if k:
                t = pltpu.roll(t, LANES - targets, 1)
            t = jnp.where(lane < targets, t, 0.0)
            u = (2.0 * couple_gain) * h * t
            cu = c * u
            around, c_around = before(u) + after(u), before(cu) + after(cu)
            change = own * u + (GAIN0 * GAIN1) * h * (c * around + c_around)
            save[k, 0, e] = change
            save[k, 1, e] = around + u
            save[k, 2, e] = c_around + cu
            rows.append(field(k, 4 + e) + change)
        sides.append(rows)

    groups = count // 8
    total = jnp.zeros((16, targets), jnp.float32)
    r = lax.broadcasted_iota(jnp.int32, total.shape, 0)
    for g in range(groups):
        both = [
            jnp.concatenate([sides[k][e][8 * g : 8 * g + 8] for e in range(excite)], axis=0)
            for k in range(2)
        ]
        for ref, left in (
            (mine, jnp.where(n == 0, both[0], both[1])),
            (theirs, jnp.where(n == 0, both[1], both[0])),
        ):
            left = left.astype(jnp.bfloat16)
            for j in range(8):
                part = nt(left, ref[:, (8 * g + j) * LANES : (8 * g + j + 1) * LANES])
                total = total + jnp.where((r & 7) == j, part, 0.0)
    first = flat[pl.ds(pl.multiple_of(w * 16, 16), 8), :] + flat[pl.ds(pl.multiple_of(w * 16 + 8, 8), 8), :]
    first = jnp.where(n == 0, first, pltpu.roll(first, LANES - targets, 1))
    traction[...] = jnp.zeros(traction.shape, jnp.float32)
    for e in range(excite):
        traction[e : e + 1, 0:targets] = (
            jnp.sum(total[8 * e : 8 * e + 8], axis=0, keepdims=True)
            + first[2 + e : 3 + e, 0:targets]
        )

    fix[...] = jnp.zeros(fix.shape, jnp.float32)
    for e in range(excite):
        for i in range(3):
            row = 2 * i + e
            fix[row : row + 1] = save[n, i, e, pl.ds(w, 1), :]
        for i in range(1, 3):
            row = 4 + 2 * i + e
            fix[row : row + 1] = jnp.where(n == 0, save[1, i, e, pl.ds(w, 1), :], 0.0)


def mend_kernel(pressure, near, fix, out):
    v = lax.axis_index("vol")
    excite, _, cells_y, cells_x = pressure.shape
    r = lax.broadcasted_iota(jnp.int32, (8, cells_x), 0)
    out[...] = pressure[...]
    for e in range(excite):
        for m in range(2):
            li = v if m == 0 else 1 - v

            def change(i, a, b):
                c, h = near[3 * m + i : 3 * m + i + 1], near[6 + 3 * m + i : 7 + 3 * m + i]
                return (GAIN0 * GAIN1) * h * (c * fix[a + e : a + e + 1] + fix[b + e : b + e + 1])

            row0 = fix[e : e + 1] if m == 0 else change(0, 2, 4)
            delta = jnp.where(r == 0, row0, jnp.where(r == 1, change(1, 2, 4), 0.0))
            out[e, li, 0:8] = pressure[e, li, 0:8] + delta
            delta = jnp.where(r == 7, change(2, 6, 8), 0.0)
            out[e, li, cells_y - 8 : cells_y] = pressure[e, li, cells_y - 8 : cells_y] + delta


def local(forcing, material_ids, materials, boundary_operator):
    vols, wides, narrows = (lax.axis_size(a) for a in ("vol", "wide", "narrow"))
    v = lax.axis_index("vol")
    excite, layers, cells_y, cells_x = forcing.shape
    assert (vols, narrows, excite, layers, cells_x) == (2, 2, 2, 2, LANES)
    assert wides % 8 == 0 and wides & (wides - 1) == 0
    tile_rows = boundary_operator.shape[0]
    targets = tile_rows // narrows
    assert tile_rows == LANES and BY * 2 * excite == 64
    width = -(-(cells_y + 2 * HALO) // LANES) * LANES
    slabs = 4 * excite + 4
    f32, bf16 = jnp.float32, jnp.bfloat16
    everyone = ("vol", "wide", "narrow")
    vmem = pl.BlockSpec(memory_space=pltpu.VMEM)

    hbm = pl.BlockSpec(memory_space=pltpu.HBM)

    def call(kernel, shapes, specs, scratch=(), limit=4, outs=None, **more):
        return pl.pallas_call(
            kernel,
            out_shape=[jax.ShapeDtypeStruct(*s) if isinstance(s, tuple) else s for s in shapes],
            in_specs=specs,
            out_specs=outs or [vmem] * len(shapes),
            scratch_shapes=list(scratch),
            compiler_params=pltpu.CompilerParams(vmem_limit_bytes=limit * 2**20),
            **more,
        )

    def swap(x, axis):
        return lax.ppermute(x, axis, [(0, 1), (1, 0)])

    def number(a, b, c):
        return (a * wides + b) * narrows + c

    def in_hbm(x):
        return pltpu.with_memory_space_constraint(x, pltpu.HBM)

    dma = pltpu.SemaphoreType.DMA
    half = slabs // 2
    f_other, id_other = swap(forcing, "vol"), swap(material_ids, "vol")
    own, edge, spread, sent, mine = call(
        own_kernel,
        [
            ((half, cells_x, width), f32),
            ((half, HALO, cells_x), f32),
            ((materials.shape[0], LANES), f32),
        ]
        + [pltpu.VMEM((targets, wides * LANES), bf16)] * 2,
        [hbm] * 4,
        [
            pltpu.VMEM(forcing.shape, f32),
            pltpu.VMEM(material_ids.shape, jnp.int32),
            pltpu.SMEM(materials.shape, f32),
            dma((5,)),
        ],
    )(in_hbm(materials), in_hbm(forcing), in_hbm(material_ids), in_hbm(boundary_operator))
    (edge,) = call(edge_kernel, [((slabs, HALO, cells_x), f32)], [vmem] * 4)(
        f_other, id_other, edge, spread
    )
    edge = swap(edge, "narrow")
    (other,) = call(other_kernel, [((half, cells_x, width), f32)], [vmem] * 3)(
        f_other, id_other, spread
    )
    used = cells_y - (width - LANES)
    odd_pairs = []
    for a in range(vols):
        for b in range(wides):
            for c in range(narrows):
                far = b + 1 if b % 2 else b - 1
                there = (far, c) if 0 <= far < wides else (b, 1 - c)
                odd_pairs.append((number(a, b, c), number(a, *there)))
    rows = cells_x + 2 * TILE
    full = (rows, width)
    many = pltpu.VMEM((4 * excite,) + full, f32)
    scratch = [pltpu.VMEM((4,) + full, f32)] + [many] * 8
    outputs = [(forcing.shape, f32), ((16, cells_x), f32)]

    def sides(own, other, edge):
        return call(
            functools.partial(side_kernel, used),
            [((slabs, HALO, width), f32)] * 2 + [((cells_x, LANES), f32)],
            [vmem] * 3,
        )(own, other, edge)

    def trade_even(even):
        return lax.ppermute(even, "wide", [(i, i ^ 1) for i in range(wides)])

    def trade_odd(odd):
        return lax.ppermute(odd, everyone, odd_pairs)

    def extend(own, other, turned):
        return call(
            functools.partial(extend_kernel, used),
            [((slabs,) + full, f32), pltpu.HBM((slabs,) + full, f32)],
            [vmem] * 3,
            [dma((slabs,))],
            outs=[vmem, hbm],
        )(own, other, turned)

    def upper(own, other, edge, operator, sent, mine):
        even, odd, turned = sides(own, other, edge)
        even = trade_even(even)
        odd = trade_odd(odd)
        ext, saved = extend(own, other, turned)
        theirs = swap(sent, "narrow")
        _, saved, trace, aux = call(
            functools.partial(sweep_kernel, cells_y // BY),
            [
                ((slabs,) + full, f32),
                pltpu.HBM((slabs,) + full, f32),
                ((wides, BY * 2 * excite, cells_x), bf16),
                ((8, cells_x), f32),
            ],
            [vmem, hbm, vmem, vmem],
            scratch + [pltpu.VMEM((excite,) + full, f32), dma((2,))],
            20,
            outs=[vmem, hbm, vmem, vmem],
            input_output_aliases={0: 0, 1: 1},
        )(ext, saved, even, odd)
        blocks = lax.all_to_all(trace, "wide", 0, 0)
        pressure, near = call(field_kernel, outputs, [vmem], scratch, 20)(saved)
        (sums,) = call(product_kernel, [((wides * narrows, 8, tile_rows), f32)], [vmem] * 3, (), 24)(
            blocks, operator, aux
        )
        blocks = lax.all_to_all(sums, ("wide", "narrow"), 0, 0)
        traction, fix = call(
            couple_kernel,
            [((8, LANES), f32), ((16, cells_x), f32)],
            [vmem] * 3,
            [pltpu.VMEM((2, 3, excite, wides, LANES), f32)],
        )(blocks.reshape(wides * narrows * 8, LANES), mine, theirs)
        return pressure, near, traction, fix

    def lower(own, other, edge, *_):
        even, odd, turned = sides(own, other, edge)
        ext, _ = extend(own, other, turned)
        even, odd, ext = lax.optimization_barrier((even, odd, ext))
        even, odd = trade_even(even), trade_odd(odd)
        _, pressure, near = call(
            lower_kernel, [((slabs,) + full, f32)] + outputs, [vmem] * 3, scratch, 20, input_output_aliases={0: 0}
        )(ext, even, odd)
        return pressure, near, jnp.zeros((8, LANES), f32), jnp.zeros((16, cells_x), f32)

    pressure, near, traction, fix = lax.cond(
        v == vols - 1, upper, lower, own, other, edge, boundary_operator, sent, mine
    )
    (pressure,) = call(mend_kernel, [(forcing.shape, f32)], [vmem] * 3)(pressure, near, fix)
    column = traction[0:2, :targets]
    first = swap(column, "vol")
    column = jnp.where(v == vols - 1, column[1:2], first[0:1])
    return pressure, column.reshape(targets, 1)


def solution(mesh):
    placed = (
        P(None, "vol", "narrow", "wide"),
        P("vol", "narrow", "wide"),
        P(),
        P("wide", "narrow"),
    )

    return jax.shard_map(
        local,
        mesh=mesh,
        in_specs=placed,
        out_specs=(P(None, "vol", "narrow", "wide"), P(("wide", "narrow"), "vol")),
        check_vma=False,
    )
```
